128 devices in a mesh: owner: 4 (over y), worker: 32 (over x, z, core).
Axes of the slice: x: 4, y: 4, z: 4, core: 2. Of those that a mesh axis runs over, the one named last changes fastest.
Arguments:
- states: float32 [262144, 512], P(('owner', 'worker')), may hold values from -3 to 3
- row_of_user: int32 [262144], replicated, may hold values from 0 to 262143, as said below
- event_users: int32 [65536], P(('owner', 'worker')), may hold values from 0 to 262143, as said below
- event_features: int32 [65536], P(('owner', 'worker')), may hold values from 0 to 4095
- feature_table: bfloat16 [4096, 512], replicated, may hold values from -6 to 6
- gate_in: bfloat16 [512, 1536], replicated, may hold values from -0.25 to 0.25
- gate_state: bfloat16 [512, 1536], replicated, may hold values from -0.25 to 0.25
- tower_in: bfloat16 [4096, 1024], P(('owner', 'worker')), may hold values from -0.1875 to 0.1875
- tower_out: bfloat16 [512, 4096], P(('owner', 'worker')), may hold values from -0.09375 to 0.09375
Outputs:
- new_states: float32 [262144, 512], P(('owner', 'worker'))
- scores: float32 [65536], P(('owner', 'worker'))
The draws below stay inside these ranges and needn't reach their ends.
Inputs may be any that keep to these rules, and one draw needn't show every extreme that they name: `row_of_user`: A permutation: each user has its own state row. `event_users`: among the 512 events of one device, at most 8 have their row (row_of_user of the user) in one device's block of 2048 rows, and for every device some block receives exactly 8 of its events.
All inputs are finite; a program needn't handle non-finite values.
Results may differ from the reference program's by a relative error of at most 0.0034.
Values may be sent and summed in bfloat16 or wider, within the bound.
A program may use at most 128 MiB of HBM per device.

```python
import math
import jax
import jax.numpy as jnp
import numpy as np
from jax import lax

S = 512
HID = 4096
FEATS = 4096
U_DEV = 2048
EV_DEV = 512
SHARDS = 128
USERS = 262144
EVENTS = 65536
MEAN_SLOTS = 4


def joint_draw(key):
    row_of_user = jax.random.permutation(jax.random.fold_in(key, 11), USERS).astype(jnp.int32)
    hot = jax.random.randint(jax.random.fold_in(key, 12), (SHARDS,), 0, 2)
    noise = jax.random.randint(jax.random.fold_in(key, 13), (SHARDS, SHARDS), 0, 1024)
    score = (noise + hot[None, :] * 1024) * SHARDS + jnp.arange(SHARDS)[None, :]
    ranked = jnp.argsort(-score, axis=1).astype(jnp.int32)
    slot = jnp.arange(EV_DEV)
    half = EV_DEV // 2
    place = jnp.where(slot < half, slot // (2 * MEAN_SLOTS), SHARDS // 4 + (slot - half) // MEAN_SLOTS)
    target = ranked[:, place]
    mixer = jax.random.randint(jax.random.fold_in(key, 14), (SHARDS, EV_DEV), 0, 4096) * EV_DEV + slot[None, :]
    order = jnp.argsort(mixer, axis=1)
    target = jnp.take_along_axis(target, order, axis=1)
    local = jax.random.randint(jax.random.fold_in(key, 15), (SHARDS, EV_DEV), 0, U_DEV)
    rows = (target * U_DEV + local).reshape(EVENTS)
    user_of_row = jnp.zeros((USERS,), jnp.int32).at[row_of_user].set(jnp.arange(USERS, dtype=jnp.int32))
    return (row_of_user, user_of_row[rows].astype(jnp.int32))


def draw_row_of_user(key, part):
    return joint_draw(key)[0]


def draw_event_users(key, part):
    return joint_draw(key)[1]


def with_ends(drawn, rng, low, high):
    dims = drawn.shape
    index_at = [jax.random.randint(jax.random.fold_in(rng, axis), (), 0, dims[axis]) for axis in range(len(dims))]
    drawn = drawn.at[tuple(index_at)].set(low)
    longest = dims.index(max(dims))
    index_at[longest] = (index_at[longest] + 1) % dims[longest]
    return drawn.at[tuple(index_at)].set(high)


def level_of(key, dims, cuts, least, high):
    def one(axis_at, blocks):
        heights = jax.random.uniform(jax.random.fold_in(jax.random.fold_in(key, 6), axis_at), (blocks,), jnp.float32, least / len(cuts), high / len(cuts))
        return jnp.repeat(jnp.exp(heights), dims[axis_at] // blocks).reshape((-1,) + (1,) * (len(dims) - axis_at - 1))

    gain = one(*cuts[0])
    for cut in cuts[1:]:
        gain = gain * one(*cut)
    return gain


def cumulative_ranks(number_of, lean):
    loads = [(1 << 20) // math.isqrt(standing ** lean) + 1 for standing in range(1, number_of + 1)]
    scale = 1 + sum(loads) // (1 << 30)
    return np.cumsum(np.array([max(1, weight // scale) for weight in loads]))


def ranked_ids(rng, shape, number_of, lean):
    listing = cumulative_ranks(number_of, lean)
    ticket = jax.random.randint(jax.random.fold_in(rng, 1), shape, 0, int(listing[number_of - 1]))
    grade = jnp.searchsorted(jnp.asarray(listing, jnp.int32), ticket, side="right")
    return jax.random.permutation(jax.random.fold_in(rng, 2), number_of)[grade].astype(jnp.int32)


def normal_values(key, extent, deviation, bound, pieces=(), held_as=jnp.bfloat16):
    drawn = jax.random.normal(key, extent, jnp.float32) * deviation
    if len(pieces) > 0:
        drawn = level_of(key, extent, pieces, -0.22, 0.18) * drawn
    return jnp.clip(drawn, min=-bound, max=bound).astype(held_as)


def setup_inputs(seed: int = 0) -> dict:
    arg_keys = jax.random.split(jax.random.key(seed), 10)
    return {
        "states": normal_values(arg_keys[0], (USERS, S), 0.5, 3.0, ((0, 128),), jnp.float32),
        "row_of_user": draw_row_of_user(jax.random.fold_in(arg_keys[9], 71), 0),
        "event_users": draw_event_users(jax.random.fold_in(arg_keys[9], 71), 0),
        "event_features": with_ends(ranked_ids(arg_keys[3], (EVENTS,), FEATS, 2), jax.random.fold_in(arg_keys[3], 3), 0, FEATS - 1).astype(jnp.int32),
        "feature_table": normal_values(arg_keys[4], (FEATS, S), 1.0, 6.0),
        "gate_in": normal_values(arg_keys[5], (S, 3 * S), S ** -0.5, 0.25),
        "gate_state": normal_values(arg_keys[6], (S, 3 * S), S ** -0.5, 0.25),
        "tower_in": normal_values(arg_keys[7], (HID, 2 * S), (2 * S) ** -0.5, 0.1875, ((0, 128),)),
        "tower_out": normal_values(arg_keys[8], (S, HID), HID ** -0.5, 0.09375, ((0, 128),)),
    }


def gru_cell(inputs, prior, gate_in, gate_state):
    gx = jnp.dot(inputs, gate_in, preferred_element_type=jnp.float32)
    gh = jnp.dot(prior, gate_state, preferred_element_type=jnp.float32)
    width = prior.shape[-1]
    reset = jax.nn.sigmoid(gx[:, :width] + gh[:, :width])
    update = jax.nn.sigmoid(gx[:, width:2 * width] + gh[:, width:2 * width])
    cand = jnp.tanh(gx[:, 2 * width:] + reset * gh[:, 2 * width:])
    return (1.0 - update) * cand + update * prior.astype(jnp.float32)

def reference(states, row_of_user, event_users, event_features, feature_table, gate_in, gate_state, tower_in, tower_out):
    rows = row_of_user[event_users]
    prior = states[rows].astype(jnp.bfloat16)
    inputs = feature_table[event_features]

    def block(pair):
        x_blk, h_blk = pair
        fresh = gru_cell(x_blk, h_blk, gate_in, gate_state)
        joined = jnp.concatenate([fresh.astype(jnp.bfloat16), x_blk], axis=1)
        hidden = jax.nn.gelu(lax.dot_general(joined, tower_in, (((1,), (1,)), ((), ())), preferred_element_type=jnp.float32)).astype(jnp.bfloat16)
        tower = lax.dot_general(hidden, tower_out, (((1,), (1,)), ((), ())), preferred_element_type=jnp.float32)
        score = lax.optimization_barrier(jnp.sum(tower * x_blk.astype(jnp.float32), axis=1)) / jnp.sqrt(jnp.float32(S))
        return (score, fresh - h_blk.astype(jnp.float32))
    scores, delta = lax.map(block, (inputs.reshape(SHARDS, EV_DEV, S), prior.reshape(SHARDS, EV_DEV, S)))
    total = jax.ops.segment_sum(delta.reshape(EVENTS, S), rows, num_segments=USERS)
    count = jax.ops.segment_sum(jnp.ones((EVENTS,), jnp.int32), rows, num_segments=USERS)
    new_states = states + total / jnp.maximum(count, 1).astype(jnp.float32)[:, None]
    return (new_states, scores.reshape(EVENTS))
```

```python
import jax
import jax.numpy as jnp
from jax import lax
from jax.sharding import PartitionSpec as P

AXES = ("owner", "worker")


def gru_cell(inputs, prior, gate_in, gate_state):
    gx = jnp.dot(inputs, gate_in, preferred_element_type=jnp.float32)
    gh = jnp.dot(prior, gate_state, preferred_element_type=jnp.float32)
    width = prior.shape[-1]
    reset = jax.nn.sigmoid(gx[:, :width] + gh[:, :width])
    update = jax.nn.sigmoid(gx[:, width : 2 * width] + gh[:, width : 2 * width])
    cand = jnp.tanh(gx[:, 2 * width :] + reset * gh[:, 2 * width :])
    return (1.0 - update) * cand + update * prior.astype(jnp.float32)


def per_device(
    states,
    row_of_user,
    event_users,
    event_features,
    feature_table,
    gate_in,
    gate_state,
    tower_in,
    tower_out,
):
    shards = lax.axis_size(AXES)
    events = event_users.shape[0]
    row_count, width = states.shape
    cap = 2 * (events // shards)
    rows = row_of_user[event_users]
    target = rows // row_count
    local = rows - target * row_count
    hits = (target[:, None] == jnp.arange(shards, dtype=jnp.int32)[None, :]).astype(jnp.int32)
    rank = jnp.sum((jnp.cumsum(hits, axis=0) - hits) * hits, axis=1)
    slot = target * cap + rank
    packed = local + row_count * event_features
    requests = jnp.full((shards * cap,), -1, jnp.int32).at[slot].set(packed).reshape(shards, cap)
    asked = lax.all_to_all(requests, AXES, split_axis=0, concat_axis=0, tiled=True).reshape(-1)
    valid = asked >= 0
    owned = jnp.where(valid, asked, 0)
    owned_feature = owned // row_count
    owned_row = owned - owned_feature * row_count
    prior = states[owned_row].astype(jnp.bfloat16)
    inputs = feature_table[owned_feature]
    fresh = gru_cell(inputs, prior, gate_in, gate_state)
    delta = fresh - prior.astype(jnp.float32)
    ids = jnp.where(valid, owned_row, row_count)
    total = jax.ops.segment_sum(delta, ids, num_segments=row_count + 1)[:row_count]
    count = jax.ops.segment_sum(valid.astype(jnp.int32), ids, num_segments=row_count + 1)[:row_count]
    new_states = states + total / jnp.maximum(count, 1).astype(jnp.float32)[:, None]
    joined = jnp.concatenate([fresh.astype(jnp.bfloat16), inputs], axis=1)
    hidden = jax.nn.gelu(
        lax.dot_general(
            joined,
            lax.all_gather(tower_in, AXES, axis=0, tiled=True),
            (((1,), (1,)), ((), ())),
            preferred_element_type=jnp.float32,
        )
    ).astype(jnp.bfloat16)
    tower = lax.dot_general(
        hidden,
        lax.all_gather(tower_out, AXES, axis=0, tiled=True),
        (((1,), (1,)), ((), ())),
        preferred_element_type=jnp.float32,
    )
    scored = jnp.sum(tower * inputs.astype(jnp.float32), axis=1) / jnp.sqrt(jnp.float32(width))
    back = lax.all_to_all(scored.reshape(shards, cap), AXES, split_axis=0, concat_axis=0, tiled=True)
    return (new_states, back.reshape(-1)[slot])


def solution(mesh):
    placed = (
        P(AXES, None),
        P(),
        P(AXES),
        P(AXES),
        P(),
        P(),
        P(),
        P(AXES, None),
        P(AXES, None),
    )
    return jax.shard_map(
        per_device,
        mesh=mesh,
        in_specs=placed,
        out_specs=(P(AXES, None), P(AXES)),
        check_vma=False,
    )
```

```python
import functools

import jax
import jax.numpy as jnp
from jax import lax
from jax.experimental import pallas as pl
from jax.experimental.pallas import tpu as pltpu
from jax.sharding import PartitionSpec as P

AXES = ("owner", "worker")
MESH = pl.DeviceIdType.MESH
RING = 4
NDEV = 128
CAP = 8
F32 = jnp.float32
BF16 = jnp.bfloat16


def iota(shape, dim):
    return lax.broadcasted_iota(jnp.int32, shape, dim)


def one_hot(hit):
    return jnp.where(hit, 1.0, 0.0).astype(BF16)


def dot(a, b):
    return jnp.dot(a, b, preferred_element_type=F32)


def dot_nt(a, b):
    return lax.dot_general(a, b, (((1,), (1,)), ((), ())), preferred_element_type=F32)


def kernel(
    ids_ref,
    table_ref,
    states_ref,
    features_ref,
    gate_in_ref,
    gate_state_ref,
    tin_ref,
    tout_ref,
    new_ref,
    score_ref,
    table,
    st,
    st16,
    feat,
    gin,
    gst,
    win,
    wout,
    raw,
    qsend,
    qrecv,
    ssend,
    srecv,
    hits,
    ranks,
    locb,
    featb,
    locr,
    joined,
    prior,
    xperm,
    dl,
    perm,
    acc,
    load_sem,
    own_sem,
    out_sem,
    a2a_sem,
    send1,
    recv1,
    send2,
    recv2,
    send3,
    recv3,
    sib_send,
    sib_recv,
):
    y = lax.axis_index("owner")
    w = lax.axis_index("worker")
    x, z, c = w // 8, (w // 2) % RING, w % 2
    me = y * 32 + w
    pos = {"x": x, "y": y, "z": z}

    def device(axis, p):
        at = dict(pos)
        at[axis] = p
        return (at["y"], at["x"] * 8 + at["z"] * 2 + c)

    sibling = (y, x * 8 + z * 2 + (1 - c))

    def remote(ref, send, recv, to, dst=None):
        return pltpu.make_async_remote_copy(
            src_ref=ref,
            dst_ref=ref if dst is None else dst,
            send_sem=send,
            recv_sem=recv,
            device_id=to,
            device_id_type=MESH,
        )

    loads = [
        pltpu.make_async_copy(src, dst, load_sem.at[i])
        for i, (src, dst) in enumerate(
            (
                (table_ref, table),
                (states_ref, st),
                (features_ref, feat),
                (gate_in_ref, gin),
                (gate_state_ref, gst),
            )
        )
    ]
    own = [
        pltpu.make_async_copy(tout_ref, raw.at[z], own_sem.at[0]),
        pltpu.make_async_copy(tin_ref.at[pl.ds(0, 16)], win.at[y, x, z, c, 0], own_sem.at[1]),
        pltpu.make_async_copy(tin_ref.at[pl.ds(16, 16)], win.at[y, x, z, c, 1], own_sem.at[2]),
    ]
    loads[0].start()

    firsts = (
        ("z", tout_ref, raw.at[z]),
        ("x", tin_ref.at[pl.ds(0, 16)], win.at[y, x, z, c, 0]),
        ("y", tin_ref.at[pl.ds(16, 16)], win.at[y, x, z, c, 1]),
    )
    stage1 = []
    for part, (axis, src, dst) in enumerate(firsts):
        for hop in (1, 3, 2):
            stage1.append(
                remote(
                    src,
                    send1.at[part, hop - 1],
                    recv1.at[part, hop - 1],
                    device(axis, (pos[axis] + hop) % RING),
                    dst,
                )
            )
    for copy in stage1:
        copy.start()
    for copy in own:
        copy.start()
    for copy in loads[1:]:
        copy.start()

    def view2(part, p, h):
        if part == 0:
            return wout.at[y, p, c, :, pl.ds(2048 * h, 2048)]
        if part == 1:
            return win.at[p, pl.ds(2 * h, 2), z, c, 0]
        return win.at[pl.ds(2 * h, 2), x, p, c, 1]

    def view3(part, p, h):
        if part == 0:
            return wout.at[p, pl.ds(2 * h, 2), c]
        if part == 1:
            return win.at[pl.ds(2 * h, 2), :, p, c, 0]
        return win.at[pl.ds(2 * h, 2), p, :, c, 1]

    class Ring:
        def __init__(self, view, axis, part, send, recv):
            p = pos[axis]
            up, down, far = (p + 1) % RING, (p + RING - 1) % RING, (p + 2) % RING
            right, left = device(axis, up), device(axis, down)

            def hop(n, block, h, to):
                return remote(view(part, block, h), send.at[part, n], recv.at[part, n], to)

            self.sends = [
                hop(0, p, 0, right),
                hop(1, p, 1, left),
                hop(2, p, 1, right),
                hop(3, p, 0, left),
                hop(4, down, 0, right),
                hop(5, up, 1, left),
            ]
            self.arrivals = [
                hop(0, down, 0, right),
                hop(1, up, 1, left),
                hop(2, down, 1, right),
                hop(3, up, 0, left),
                hop(4, far, 0, right),
                hop(5, far, 1, left),
            ]

        def begin(self):
            for n in range(4):
                self.sends[n].start()

        def forward(self):
            for n in (0, 1):
                self.arrivals[n].wait_recv()
                self.sends[4 + n].start()

        def arrive(self, *which):
            for n in which:
                self.arrivals[n].wait_recv()

        def drain(self):
            for copy in self.sends:
                copy.wait_send()

    ids = ids_ref[...].astype(F32)
    both = jnp.where(
        iota((128, 512), 0) < 64,
        jnp.broadcast_to(ids[0:1], (128, 512)),
        jnp.broadcast_to(ids[1:2], (128, 512)),
    )
    both = both.T
    user = both[:, 0:1].astype(jnp.int32)
    feature = both[:, 64:65].astype(jnp.int32)
    user_b = jnp.broadcast_to(user, (512, 128))
    lanes = iota((512, 128), 1)
    loads[0].wait()
    rows3 = jnp.zeros((512, 384), F32)
    for k in range(4):
        piece = table[pl.ds(512 * k, 512), :]
        parts = [piece & 255, (piece >> 8) & 255, piece >> 16]
        bytes3 = jnp.concatenate([v.astype(F32).astype(BF16) for v in parts], axis=1)
        pick = one_hot(iota((512, 512), 1) + 512 * k == (user >> 7))
        rows3 = rows3 + dot(pick, bytes3)
    found = rows3[:, 0:128] + 256.0 * rows3[:, 128:256] + 65536.0 * rows3[:, 256:384]
    row = jnp.sum(jnp.where(lanes == (user_b & 127), found, 0.0), axis=1, keepdims=True)
    row = row.astype(jnp.int32)
    hit = lanes == (row >> 11)
    hit16 = one_hot(hit)
    hits[...] = hit16
    before = one_hot(iota((512, 512), 1) < iota((512, 512), 0))
    rank = jnp.sum(jnp.where(hit, dot(before, hit16), 0.0), axis=1, keepdims=True)
    rank_b = jnp.broadcast_to(rank.astype(jnp.int32), (512, 128))
    ranks[...] = rank_b
    local = (row & 2047) + 1
    part = lanes // CAP
    value = jnp.where(
        part == 0,
        local & 255,
        jnp.where(part == 1, local >> 8, jnp.where(part == 2, feature & 255, feature >> 8)),
    )
    value = jnp.where((lanes % CAP == rank_b) & (part < 4), value, 0).astype(F32).astype(BF16)
    requests = dot(jnp.where(hit, 1.0, 0.0).T.astype(BF16), value)
    requests = requests + 256.0 * pltpu.roll(requests, 128 - CAP, 1)

    def exchange(values, send_ref, recv_ref, n):
        send_ref[...] = values.reshape(NDEV, 1, 128)

        @pl.loop(1, NDEV)
        def _(s):
            to = lax.rem(me + s, NDEV)
            remote(
                send_ref.at[to],
                a2a_sem.at[n],
                a2a_sem.at[n + 1],
                (to // 32, lax.rem(to, 32)),
                recv_ref.at[me],
            ).start()

        recv_ref[me] = send_ref[me]

    def all_but_one(ref, n):
        return pltpu.make_async_copy(ref.at[pl.ds(0, NDEV - 1)], ref.at[pl.ds(0, NDEV - 1)], a2a_sem.at[n])

    exchange(requests, qsend, qrecv, 0)

    for copy in own:
        copy.wait()
    for copy in stage1:
        copy.wait_recv()
    wout[y, x, c] = jnp.concatenate([raw[i].astype(F32) for i in range(RING)], axis=0).astype(BF16)
    second = [
        Ring(view2, axis, part, send2, recv2) for part, axis in enumerate(("x", "y", "z"))
    ]
    for ring in second:
        ring.begin()

    loads[1].wait()
    for k in range(4):
        st16[pl.ds(512 * k, 512), :] = st[pl.ds(512 * k, 512), :].astype(BF16)
    o = iota((512, 512), 1)
    o = (o - (o & 31)) + ((o >> 2) & 3) * 8 + ((o >> 4) & 1) * 4 + (o & 3)
    perm[...] = one_hot(iota((512, 512), 0) == o)

    for ring in second:
        ring.forward()

    all_but_one(qrecv, 1).wait()
    asked = qrecv[...].reshape(NDEV, 128)
    for k in range(CAP):
        locb[k] = jnp.broadcast_to(asked[:, k : k + 1], (NDEV, 128))
        featb[k] = jnp.broadcast_to(asked[:, 16 + k : 17 + k], (NDEV, 128))
    flipped = asked.T
    for k in range(CAP):
        locr[:, k * 128 : (k + 1) * 128] = jnp.broadcast_to(flipped[k : k + 1], (8, 128))

    def take_prior(m):
        at = locb[pl.ds(4 * m, 4)].reshape(512, 128)[:, 0:1].astype(jnp.int32)
        pick = one_hot(iota((512, 2048), 1) + 1 == at)
        prior[pl.ds(pl.multiple_of(512 * m, 512), 512), :] = dot(pick, st16[...]).astype(BF16)

    def take_inputs(m):
        at = featb[pl.ds(4 * m, 4)].reshape(512, 128)[:, 0:1].astype(jnp.int32)
        pick = one_hot(iota((512, 4096), 1) == at)
        joined[pl.ds(pl.multiple_of(512 * m, 512), 512), 512:1024] = dot(pick, feat[...]).astype(BF16)

    @pl.loop(0, 2)
    def _(m):
        take_prior(m)

    for ring in second:
        ring.arrive(2, 3, 4, 5)
    third = [Ring(view3, axis, part, send3, recv3) for part, axis in enumerate(("y", "z", "x"))]
    for ring in third:
        ring.begin()

    def to_sibling(part, axis, n):
        p = pos[axis]
        block = (p, (p + RING - 1) % RING, (p + 1) % RING, (p + 2) % RING)[n]
        if part == 0:
            ref = wout.at[block, :, c]
        elif part == 1:
            ref = win.at[:, :, block, c, 0]
        else:
            ref = win.at[:, block, :, c, 1]
        return remote(ref, sib_send.at[part, n], sib_recv.at[part, n], sibling)

    lasts = [[to_sibling(part, axis, n) for n in range(4)] for part, axis in enumerate(("y", "z", "x"))]
    for part in range(3):
        lasts[part][0].start()

    loads[2].wait()

    @pl.loop(0, 2)
    def _(m):
        take_inputs(m)

    for ring in third:
        ring.forward()

    loads[3].wait()
    loads[4].wait()

    @pl.loop(0, 4)
    def _(m):
        at = pl.ds(pl.multiple_of(256 * m, 256), 256)
        inputs = joined[at, 512:1024]
        old = prior[at, :]
        gx = dot(inputs, gin[...])
        gh = dot(old, gst[...])
        reset = 0.5 * jnp.tanh(0.5 * (gx[:, 0:512] + gh[:, 0:512])) + 0.5
        update = 0.5 * jnp.tanh(0.5 * (gx[:, 512:1024] + gh[:, 512:1024])) + 0.5
        cand = jnp.tanh(gx[:, 1024:1536] + reset * gh[:, 1024:1536])
        before = old.astype(F32)
        fresh = (1.0 - update) * cand + update * before
        joined[at, 0:512] = fresh.astype(BF16)
        delta = fresh - before
        high = delta.astype(BF16)
        dl[at, 0:512] = high
        dl[at, 512:1024] = (delta - high.astype(F32)).astype(BF16)
        xperm[at, :] = dot(inputs, perm[...]).astype(BF16)

    for part in range(3):
        third[part].arrive(2, 3)
        lasts[part][1].start()
        lasts[part][2].start()

    @pl.loop(0, 4)
    def _(m):
        at = pl.ds(pl.multiple_of(512 * m, 512), 512)
        owned = jnp.broadcast_to(locr[0:1, :], (512, 1024)).astype(jnp.int32)
        mine = iota((512, 1024), 0) + (512 * m + 1) == owned
        total2 = dot(one_hot(mine), dl[...])
        count = jnp.sum(jnp.where(mine, 1.0, 0.0), axis=1, keepdims=True)
        total = total2[:, 0:512] + total2[:, 512:1024]
        st[at, :] = st[at, :] + total / jnp.maximum(count, 1.0)

    result = pltpu.make_async_copy(st, new_ref, out_sem)
    result.start()

    for part in range(3):
        third[part].arrive(4, 5)
        lasts[part][3].start()
    for part in range(3):
        for copy in lasts[part]:
            copy.wait_recv()

    acc[...] = jnp.zeros_like(acc)

    @pl.loop(0, 16)
    def _(j):
        hid = pl.ds(pl.multiple_of(256 * j, 256), 256)
        first = win[j // RING, lax.rem(j, RING)].reshape(256, 1024)
        second_w = wout[:, :, :, :, hid].reshape(512, 256)

        @pl.loop(0, 2)
        def _(m):
            at = pl.ds(pl.multiple_of(512 * m, 512), 512)
            v = dot_nt(joined[at, :], first)
            inner = 0.7978845608028654 * (v + 0.044715 * (v * v * v))
            hidden = (v * (0.5 * (1.0 + jnp.tanh(inner)))).astype(BF16).astype(F32)
            prod = hidden * dot(xperm[at, :], second_w)
            acc[at, :] += prod[:, 0:128] + prod[:, 128:256]

    lane = iota((NDEV, 128), 1)
    scores = jnp.zeros((NDEV, 128), F32)
    for k in range(CAP):
        s = jnp.sum(acc[k * 128 : (k + 1) * 128, :], axis=1, keepdims=True)
        scores = jnp.where(lane == k, s, scores)
    scores = scores * (1.0 / (512.0**0.5))
    exchange(scores, ssend, srecv, 2)

    for copy in stage1:
        copy.wait_send()
    for ring in second + third:
        ring.drain()
    for part in range(3):
        for copy in lasts[part]:
            copy.wait_send()
    all_but_one(qsend, 0).wait()
    result.wait()

    all_but_one(srecv, 3).wait()
    back = srecv[...].reshape(NDEV, 128)
    high = back.astype(BF16)
    rest = back - high.astype(F32)
    middle = rest.astype(BF16)
    low = (rest - middle.astype(F32)).astype(BF16)
    three = jnp.concatenate([high, middle, low], axis=1)
    got = dot(hits[...], three)
    got = got[:, 0:128] + got[:, 128:256] + got[:, 256:384]
    picked = jnp.where(iota((512, 128), 1) == ranks[...], got, 0.0)
    score = jnp.sum(picked, axis=1, keepdims=True)
    score_ref[...] = jnp.broadcast_to(score, (512, 128)).T[0:1, :]
    all_but_one(ssend, 2).wait()


def per_device(
    states,
    row_of_user,
    event_users,
    event_features,
    feature_table,
    gate_in,
    gate_state,
    tower_in,
    tower_out,
):
    ids = jnp.stack([event_users, event_features])
    table = row_of_user.reshape(2048, 128)
    anywhere = pl.BlockSpec(memory_space=pl.ANY)
    vmem = pl.BlockSpec(memory_space=pltpu.VMEM)
    dma = pltpu.SemaphoreType.DMA
    new_states, scores = pl.pallas_call(
        kernel,
        out_shape=(
            jax.ShapeDtypeStruct((2048, 512), F32),
            jax.ShapeDtypeStruct((1, 512), F32),
        ),
        in_specs=[vmem] + [anywhere] * 7,
        out_specs=(anywhere, vmem),
        scratch_shapes=[
            pltpu.VMEM((2048, 128), jnp.int32),
            pltpu.VMEM((2048, 512), F32),
            pltpu.VMEM((2048, 512), BF16),
            pltpu.VMEM((4096, 512), BF16),
            pltpu.VMEM((512, 1536), BF16),
            pltpu.VMEM((512, 1536), BF16),
            pltpu.VMEM((4, 4, 4, 2, 2, 16, 1024), BF16),
            pltpu.VMEM((4, 4, 2, 16, 4096), BF16),
            pltpu.VMEM((4, 4, 4096), BF16),
            pltpu.VMEM((128, 1, 128), F32),
            pltpu.VMEM((128, 1, 128), F32),
            pltpu.VMEM((128, 1, 128), F32),
            pltpu.VMEM((128, 1, 128), F32),
            pltpu.VMEM((512, 128), BF16),
            pltpu.VMEM((512, 128), jnp.int32),
            pltpu.VMEM((8, 128, 128), F32),
            pltpu.VMEM((8, 128, 128), F32),
            pltpu.VMEM((8, 1024), F32),
            pltpu.VMEM((1024, 1024), BF16),
            pltpu.VMEM((1024, 512), BF16),
            pltpu.VMEM((1024, 512), BF16),
            pltpu.VMEM((1024, 1024), BF16),
            pltpu.VMEM((512, 512), BF16),
            pltpu.VMEM((1024, 128), F32),
            dma((5,)),
            dma((3,)),
            dma,
            dma((4,)),
            dma((3, 3)),
            dma((3, 3)),
            dma((3, 6)),
            dma((3, 6)),
            dma((3, 6)),
            dma((3, 6)),
            dma((3, 4)),
            dma((3, 4)),
        ],
        compiler_params=pltpu.CompilerParams(has_side_effects=True, vmem_limit_bytes=60 * 1024 * 1024),
    )(ids, table, states, feature_table, gate_in, gate_state, tower_in, tower_out)
    return new_states, scores.reshape(512)


def solution(mesh):
    placed = (
        P(AXES, None),
        P(),
        P(AXES),
        P(AXES),
        P(),
        P(),
        P(),
        P(AXES, None),
        P(AXES, None),
    )
    return jax.shard_map(
        per_device,
        mesh=mesh,
        in_specs=placed,
        out_specs=(P(AXES, None), P(AXES)),
        check_vma=False,
    )
```

```python
import functools

import jax
import jax.numpy as jnp
from jax import lax
from jax.experimental import pallas as pl
from jax.experimental.pallas import tpu as pltpu
from jax.sharding import PartitionSpec as P

AXES = ("owner", "worker")
MESH = pl.DeviceIdType.MESH
RING = 4
NDEV = 128
CAP = 8
F32 = jnp.float32
BF16 = jnp.bfloat16


def iota(shape, dim):
    return lax.broadcasted_iota(jnp.int32, shape, dim)


def one_hot(hit):
    return jnp.where(hit, 1.0, 0.0).astype(BF16)


def dot(a, b):
    return jnp.dot(a, b, preferred_element_type=F32)


def dot_nt(a, b):
    return lax.dot_general(a, b, (((1,), (1,)), ((), ())), preferred_element_type=F32)


def kernel(
    ids_ref,
    table_ref,
    states_ref,
    features_ref,
    gate_in_ref,
    gate_state_ref,
    tin_ref,
    tout_ref,
    new_ref,
    score_ref,
    table,
    st,
    st16,
    feat,
    gin,
    gst,
    win,
    wout,
    raw,
    qsend,
    qmid,
    qrecv,
    ssend,
    smid,
    srecv,
    hits,
    ranks,
    locb,
    featb,
    locr,
    joined,
    prior,
    xperm,
    dl,
    perm,
    hidden,
    acc,
    load_sem,
    own_sem,
    out_sem,
    a2a_sem,
    send1,
    recv1,
    send2,
    recv2,
    send3,
    recv3,
    sib_send,
    sib_recv,
):
    y = lax.axis_index("owner")
    w = lax.axis_index("worker")
    x, z, c = w // 8, (w // 2) % RING, w % 2
    pos = {"x": x, "y": y, "z": z}
    yx, zc = y * RING + x, z * 2 + c

    def device(axis, p):
        at = dict(pos)
        at[axis] = p
        return (at["y"], at["x"] * 8 + at["z"] * 2 + c)

    sibling = (y, x * 8 + z * 2 + (1 - c))

    def to_plane(p):
        return (p // RING, lax.rem(p, RING) * 8 + zc)

    def to_row(p):
        return (y, x * 8 + p)

    def remote(ref, send, recv, to, dst=None):
        return pltpu.make_async_remote_copy(
            src_ref=ref,
            dst_ref=ref if dst is None else dst,
            send_sem=send,
            recv_sem=recv,
            device_id=to,
            device_id_type=MESH,
        )

    loads = [
        pltpu.make_async_copy(src, dst, load_sem.at[i])
        for i, (src, dst) in enumerate(
            (
                (table_ref, table),
                (states_ref, st),
                (features_ref, feat),
                (gate_in_ref, gin),
                (gate_state_ref, gst),
            )
        )
    ]
    own = [
        pltpu.make_async_copy(tout_ref, raw.at[z], own_sem.at[0]),
        pltpu.make_async_copy(tin_ref.at[pl.ds(0, 16)], win.at[y, x, z, c, 0], own_sem.at[1]),
        pltpu.make_async_copy(tin_ref.at[pl.ds(16, 16)], win.at[y, x, z, c, 1], own_sem.at[2]),
    ]
    for copy in loads + own:
        copy.start()

    entry = pltpu.get_barrier_semaphore()

    @pl.loop(1, 16)
    def _(s):
        pl.semaphore_signal(entry, 1, device_id=to_plane(lax.rem(yx + s, 16)), device_id_type=MESH)

    @pl.loop(1, 8)
    def _(s):
        pl.semaphore_signal(entry, 1, device_id=to_row(lax.rem(zc + s, 8)), device_id_type=MESH)

    firsts = (
        ("z", tout_ref, raw.at[z]),
        ("x", tin_ref.at[pl.ds(0, 16)], win.at[y, x, z, c, 0]),
        ("y", tin_ref.at[pl.ds(16, 16)], win.at[y, x, z, c, 1]),
    )
    stage1 = []
    for part, (axis, src, dst) in enumerate(firsts):
        for hop in (1, 3, 2):
            stage1.append(
                remote(
                    src,
                    send1.at[part, hop - 1],
                    recv1.at[part, hop - 1],
                    device(axis, (pos[axis] + hop) % RING),
                    dst,
                )
            )
    pl.semaphore_wait(entry, 22)
    for copy in stage1:
        copy.start()

    stage2 = []
    for part, axis in enumerate(("x", "y", "z")):
        block = (wout.at[y, x, c], win.at[y, :, z, c, 0], win.at[:, x, z, c, 1])[part]
        for hop in (1, 3, 2):
            to = device(axis, (pos[axis] + hop) % RING)
            stage2.append(remote(block, send2.at[part, hop - 1], recv2.at[part, hop - 1], to))

    def view3(part, p, h):
        if part == 0:
            return wout.at[p, pl.ds(2 * h, 2), c]
        if part == 1:
            return win.at[pl.ds(2 * h, 2), :, p, c, 0]
        return win.at[pl.ds(2 * h, 2), p, :, c, 1]

    class Ring:
        def __init__(self, view, axis, part, send, recv):
            p = pos[axis]
            up, down, far = (p + 1) % RING, (p + RING - 1) % RING, (p + 2) % RING
            right, left = device(axis, up), device(axis, down)

            def hop(n, block, h, to):
                return remote(view(part, block, h), send.at[part, n], recv.at[part, n], to)

            self.sends = [
                hop(0, p, 0, right),
                hop(1, p, 1, left),
                hop(2, p, 1, right),
                hop(3, p, 0, left),
                hop(4, down, 0, right),
                hop(5, up, 1, left),
            ]
            self.arrivals = [
                hop(0, down, 0, right),
                hop(1, up, 1, left),
                hop(2, down, 1, right),
                hop(3, up, 0, left),
                hop(4, far, 0, right),
                hop(5, far, 1, left),
            ]

        def begin(self):
            for n in range(4):
                self.sends[n].start()

        def forward(self):
            for n in (0, 1):
                self.arrivals[n].wait_recv()
                self.sends[4 + n].start()

        def arrive(self, *which):
            for n in which:
                self.arrivals[n].wait_recv()

        def drain(self):
            for copy in self.sends:
                copy.wait_send()

    ids = ids_ref[...].astype(F32)
    both = jnp.where(
        iota((128, 512), 0) < 64,
        jnp.broadcast_to(ids[0:1], (128, 512)),
        jnp.broadcast_to(ids[1:2], (128, 512)),
    )
    both = both.T
    user = both[:, 0:1].astype(jnp.int32)
    feature = both[:, 64:65].astype(jnp.int32)
    user_b = jnp.broadcast_to(user, (512, 128))
    lanes = iota((512, 128), 1)
    loads[0].wait()
    rows3 = jnp.zeros((512, 384), F32)
    for k in range(4):
        piece = table[pl.ds(512 * k, 512), :]
        parts = [piece & 255, (piece >> 8) & 255, piece >> 16]
        bytes3 = jnp.concatenate([v.astype(F32).astype(BF16) for v in parts], axis=1)
        pick = one_hot(iota((512, 512), 1) + 512 * k == (user >> 7))
        rows3 = rows3 + dot(pick, bytes3)
    found = rows3[:, 0:128] + 256.0 * rows3[:, 128:256] + 65536.0 * rows3[:, 256:384]
    row = jnp.sum(jnp.where(lanes == (user_b & 127), found, 0.0), axis=1, keepdims=True)
    row = row.astype(jnp.int32)
    for copy in own:
        copy.wait()
    for copy in stage1:
        copy.wait_recv()
    wout[y, x, c] = jnp.concatenate([raw[i].astype(F32) for i in range(RING)], axis=0).astype(BF16)
    for copy in stage2:
        copy.start()

    hit = lanes == (row >> 11)
    hit16 = one_hot(hit)
    hits[...] = hit16
    before = one_hot(iota((512, 512), 1) < iota((512, 512), 0))
    rank = jnp.sum(jnp.where(hit, dot(before, hit16), 0.0), axis=1, keepdims=True)
    rank_b = jnp.broadcast_to(rank.astype(jnp.int32), (512, 128))
    ranks[...] = rank_b
    local = (row & 2047) + 1
    part = lanes // CAP
    value = jnp.where(
        part == 0,
        local & 255,
        jnp.where(part == 1, local >> 8, jnp.where(part == 2, feature & 255, feature >> 8)),
    )
    value = jnp.where((lanes % CAP == rank_b) & (part < 4), value, 0).astype(F32).astype(BF16)
    requests = dot(jnp.where(hit, 1.0, 0.0).T.astype(BF16), value)
    requests = requests + 256.0 * pltpu.roll(requests, 128 - CAP, 1)

    def spread(src, dst, mine, count, n, to):
        @pl.loop(1, count)
        def _(s):
            p = lax.rem(mine + s, count)
            remote(src(p), a2a_sem.at[n], a2a_sem.at[n + 1], to(p), dst.at[mine]).start()

    def settle(ref, count, n):
        block = ref.at[pl.ds(0, count - 1)]
        pltpu.make_async_copy(block, block, a2a_sem.at[n]).wait()

    qsend[...] = requests.reshape(16, 8, 1, 128)
    spread(lambda p: qsend.at[p], qmid, yx, 16, 0, to_plane)
    qmid[yx] = qsend[yx]

    loads[1].wait()
    for k in range(4):
        st16[pl.ds(512 * k, 512), :] = st[pl.ds(512 * k, 512), :].astype(BF16)
    o = iota((512, 512), 1)
    o = (o - (o & 31)) + ((o >> 2) & 3) * 8 + ((o >> 4) & 1) * 4 + (o & 3)
    perm[...] = one_hot(iota((512, 512), 0) == o)

    settle(qmid, 16, 1)
    spread(lambda p: qmid.at[:, p], qrecv, zc, 8, 2, to_row)
    qrecv[zc] = qmid[:, zc]

    for copy in stage2:
        copy.wait_recv()
    third = [Ring(view3, axis, part, send3, recv3) for part, axis in enumerate(("y", "z", "x"))]
    for ring in third:
        ring.begin()

    def to_sibling(part, axis, n):
        p = pos[axis]
        block = (p, (p + RING - 1) % RING, (p + 1) % RING, (p + 2) % RING)[n]
        if part == 0:
            ref = wout.at[block, :, c]
        elif part == 1:
            ref = win.at[:, :, block, c, 0]
        else:
            ref = win.at[:, block, :, c, 1]
        return remote(ref, sib_send.at[part, n], sib_recv.at[part, n], sibling)

    lasts = [[to_sibling(part, axis, n) for n in range(4)] for part, axis in enumerate(("y", "z", "x"))]
    for part in range(3):
        lasts[part][0].start()

    settle(qrecv, 8, 3)
    asked = qrecv[...].reshape(NDEV, 128)
    for k in range(CAP):
        locb[k] = jnp.broadcast_to(asked[:, k : k + 1], (NDEV, 128))
        featb[k] = jnp.broadcast_to(asked[:, 16 + k : 17 + k], (NDEV, 128))
    flipped = asked.T
    for k in range(CAP):
        locr[:, k * 128 : (k + 1) * 128] = jnp.broadcast_to(flipped[k : k + 1], (8, 128))

    def take_prior(m):
        at = locb[pl.ds(4 * m, 4)].reshape(512, 128)[:, 0:1].astype(jnp.int32)
        pick = one_hot(iota((512, 2048), 1) + 1 == at)
        prior[pl.ds(pl.multiple_of(512 * m, 512), 512), :] = dot(pick, st16[...]).astype(BF16)

    def take_inputs(m):
        at = featb[pl.ds(4 * m, 4)].reshape(512, 128)[:, 0:1].astype(jnp.int32)
        pick = one_hot(iota((512, 4096), 1) == at)
        joined[pl.ds(pl.multiple_of(512 * m, 512), 512), 512:1024] = dot(pick, feat[...]).astype(BF16)

    @pl.loop(0, 2)
    def _(m):
        take_prior(m)

    for ring in third:
        ring.forward()

    for copy in loads[2:]:
        copy.wait()

    @pl.loop(0, 2)
    def _(m):
        take_inputs(m)

    for part in range(3):
        third[part].arrive(2, 3)
        lasts[part][1].start()
        lasts[part][2].start()

    @pl.loop(0, 4)
    def _(m):
        at = pl.ds(pl.multiple_of(256 * m, 256), 256)
        inputs = joined[at, 512:1024]
        old = prior[at, :]
        gx = dot(inputs, gin[...])
        gh = dot(old, gst[...])
        reset = 0.5 * jnp.tanh(0.5 * (gx[:, 0:512] + gh[:, 0:512])) + 0.5
        update = 0.5 * jnp.tanh(0.5 * (gx[:, 512:1024] + gh[:, 512:1024])) + 0.5
        cand = jnp.tanh(gx[:, 1024:1536] + reset * gh[:, 1024:1536])
        before = old.astype(F32)
        fresh = (1.0 - update) * cand + update * before
        joined[at, 0:512] = fresh.astype(BF16)
        delta = fresh - before
        high = delta.astype(BF16)
        dl[at, 0:512] = high
        dl[at, 512:1024] = (delta - high.astype(F32)).astype(BF16)
        xperm[at, :] = dot(inputs, perm[...]).astype(BF16)

    for part in range(3):
        third[part].arrive(4, 5)
        lasts[part][3].start()

    def update(m):
        at = pl.ds(pl.multiple_of(512 * m, 512), 512)
        owned = jnp.broadcast_to(locr[0:1, :], (512, 1024)).astype(jnp.int32)
        mine = iota((512, 1024), 0) + (512 * m + 1) == owned
        total2 = dot(one_hot(mine), dl[...])
        count = jnp.sum(jnp.where(mine, 1.0, 0.0), axis=1, keepdims=True)
        total = total2[:, 0:512] + total2[:, 512:1024]
        st[at, :] = st[at, :] + total / jnp.maximum(count, 1.0)

    @pl.loop(0, 2)
    def _(m):
        update(m)

    for part in range(3):
        for copy in lasts[part]:
            copy.wait_recv()

    @pl.loop(0, 16)
    def _(j):
        hid = pl.ds(pl.multiple_of(256 * j, 256), 256)
        first = win[j // RING, lax.rem(j, RING)].reshape(256, 1024)
        for m in range(2):
            at = pl.ds(512 * m, 512)
            v = dot_nt(joined[at, :], first)
            inner = v * (0.7978845608028654 + 0.035677408136300125 * (v * v))
            hidden[at, hid] = (v + v * jnp.tanh(inner)).astype(BF16)

    @pl.loop(0, 4)
    def _(m):
        at = pl.ds(pl.multiple_of(256 * m, 256), 256)
        tower = dot_nt(hidden[at, :], wout[...].reshape(512, 4096))
        prod = tower * xperm[at, :].astype(F32)
        acc[at, :] = (prod[:, 0:128] + prod[:, 128:256]) + (prod[:, 256:384] + prod[:, 384:512])

    lane = iota((NDEV, 128), 1)
    scores = jnp.zeros((NDEV, 128), F32)
    for k in range(CAP):
        s = jnp.sum(acc[k * 128 : (k + 1) * 128, :], axis=1, keepdims=True)
        scores = jnp.where(lane == k, s, scores)
    scores = scores * (0.5 / (512.0**0.5))
    ssend[...] = scores.reshape(8, 16, 1, 128)
    spread(lambda p: ssend.at[p], smid, zc, 8, 4, to_row)
    smid[zc] = ssend[zc]

    for copy in stage1:
        copy.wait_send()
    for copy in stage2:
        copy.wait_send()
    for ring in third:
        ring.drain()
    for part in range(3):
        for copy in lasts[part]:
            copy.wait_send()
    settle(qsend, 16, 0)
    settle(qrecv, 8, 2)
    update(2)
    settle(smid, 8, 5)
    spread(lambda p: smid.at[:, p], srecv, yx, 16, 6, to_plane)
    srecv[yx] = smid[:, yx]
    update(3)
    result = pltpu.make_async_copy(st, new_ref, out_sem)
    result.start()

    settle(srecv, 16, 7)
    back = srecv[...].reshape(NDEV, 128)
    high = back.astype(BF16)
    rest = back - high.astype(F32)
    middle = rest.astype(BF16)
    low = (rest - middle.astype(F32)).astype(BF16)
    three = jnp.concatenate([high, middle, low], axis=1)
    got = dot(hits[...], three)
    got = got[:, 0:128] + got[:, 128:256] + got[:, 256:384]
    picked = jnp.where(iota((512, 128), 1) == ranks[...], got, 0.0)
    score = jnp.sum(picked, axis=1, keepdims=True)
    score_ref[...] = jnp.broadcast_to(score, (512, 128)).T[0:1, :]
    settle(ssend, 8, 4)
    settle(srecv, 16, 6)
    result.wait()


def per_device(
    states,
    row_of_user,
    event_users,
    event_features,
    feature_table,
    gate_in,
    gate_state,
    tower_in,
    tower_out,
):
    ids = jnp.stack([event_users, event_features])
    table = row_of_user.reshape(2048, 128)
    anywhere = pl.BlockSpec(memory_space=pl.ANY)
    vmem = pl.BlockSpec(memory_space=pltpu.VMEM)
    dma = pltpu.SemaphoreType.DMA
    new_states, scores = pl.pallas_call(
        kernel,
        out_shape=(
            jax.ShapeDtypeStruct((2048, 512), F32),
            jax.ShapeDtypeStruct((1, 512), F32),
        ),
        in_specs=[vmem] + [anywhere] * 7,
        out_specs=(anywhere, vmem),
        scratch_shapes=[
            pltpu.VMEM((2048, 128), jnp.int32),
            pltpu.VMEM((2048, 512), F32),
            pltpu.VMEM((2048, 512), BF16),
            pltpu.VMEM((4096, 512), BF16),
            pltpu.VMEM((512, 1536), BF16),
            pltpu.VMEM((512, 1536), BF16),
            pltpu.VMEM((4, 4, 4, 2, 2, 16, 1024), BF16),
            pltpu.VMEM((4, 4, 2, 16, 4096), BF16),
            pltpu.VMEM((4, 4, 4096), BF16),
            pltpu.VMEM((16, 8, 1, 128), F32),
            pltpu.VMEM((16, 8, 1, 128), F32),
            pltpu.VMEM((8, 16, 1, 128), F32),
            pltpu.VMEM((8, 16, 1, 128), F32),
            pltpu.VMEM((8, 16, 1, 128), F32),
            pltpu.VMEM((16, 8, 1, 128), F32),
            pltpu.VMEM((512, 128), BF16),
            pltpu.VMEM((512, 128), jnp.int32),
            pltpu.VMEM((8, 128, 128), F32),
            pltpu.VMEM((8, 128, 128), F32),
            pltpu.VMEM((8, 1024), F32),
            pltpu.VMEM((1024, 1024), BF16),
            pltpu.VMEM((1024, 512), BF16),
            pltpu.VMEM((1024, 512), BF16),
            pltpu.VMEM((1024, 1024), BF16),
            pltpu.VMEM((512, 512), BF16),
            pltpu.VMEM((1024, 4096), BF16),
            pltpu.VMEM((1024, 128), F32),
            dma((5,)),
            dma((3,)),
            dma,
            dma((8,)),
            dma((3, 3)),
            dma((3, 3)),
            dma((3, 3)),
            dma((3, 3)),
            dma((3, 6)),
            dma((3, 6)),
            dma((3, 4)),
            dma((3, 4)),
        ],
        compiler_params=pltpu.CompilerParams(
            collective_id=0, has_side_effects=True, vmem_limit_bytes=60 * 1024 * 1024
        ),
    )(ids, table, states, feature_table, gate_in, gate_state, tower_in, tower_out)
    return new_states, scores.reshape(512)


def solution(mesh):
    placed = (
        P(AXES, None),
        P(),
        P(AXES),
        P(AXES),
        P(),
        P(),
        P(),
        P(AXES, None),
        P(AXES, None),
    )
    return jax.shard_map(
        per_device,
        mesh=mesh,
        in_specs=placed,
        out_specs=(P(AXES, None), P(AXES)),
        check_vma=False,
    )
```

```python
import functools

import jax
import jax.numpy as jnp
from jax import lax
from jax.experimental import pallas as pl
from jax.experimental.pallas import tpu as pltpu
from jax.sharding import PartitionSpec as P

AXES = ("owner", "worker")
MESH = pl.DeviceIdType.MESH
RING = 4
NDEV = 128
CAP = 8
F32 = jnp.float32
BF16 = jnp.bfloat16


def iota(shape, dim):
    return lax.broadcasted_iota(jnp.int32, shape, dim)


def one_hot(hit):
    return jnp.where(hit, 1.0, 0.0).astype(BF16)


def dot(a, b):
    return jnp.dot(a, b, preferred_element_type=F32)


def dot_nt(a, b):
    return lax.dot_general(a, b, (((1,), (1,)), ((), ())), preferred_element_type=F32)


def kernel(
    users_ref,
    feats_ref,
    table_ref,
    states_ref,
    features_ref,
    gate_in_ref,
    gate_state_ref,
    tin_ref,
    tout_ref,
    delta_ref,
    slots_ref,
    score_ref,
    table,
    st,
    st16,
    feat,
    gin,
    gst,
    win,
    wout,
    raw,
    qsend,
    qmid,
    qrecv,
    ssend,
    smid,
    srecv,
    hits,
    ranks,
    locb,
    featb,
    locr,
    joined,
    prior,
    xperm,
    dl,
    perm,
    hidden,
    acc,
    load_sem,
    own_sem,
    out_sem,
    a2a_sem,
    send1,
    recv1,
    send2,
    recv2,
    send3,
    recv3,
    sib_send,
    sib_recv,
):
    y = lax.axis_index("owner")
    w = lax.axis_index("worker")
    x, z, c = w // 8, (w // 2) % RING, w % 2
    pos = {"x": x, "y": y, "z": z}
    yx, zc = y * RING + x, z * 2 + c

    def device(axis, p):
        at = dict(pos)
        at[axis] = p
        return (at["y"], at["x"] * 8 + at["z"] * 2 + c)

    sibling = (y, x * 8 + z * 2 + (1 - c))

    def to_plane(p):
        return (p // RING, lax.rem(p, RING) * 8 + zc)

    def to_row(p):
        return (y, x * 8 + p)

    def remote(ref, send, recv, to, dst=None):
        return pltpu.make_async_remote_copy(
            src_ref=ref,
            dst_ref=ref if dst is None else dst,
            send_sem=send,
            recv_sem=recv,
            device_id=to,
            device_id_type=MESH,
        )

    loads = [
        pltpu.make_async_copy(src, dst, load_sem.at[i])
        for i, (src, dst) in enumerate(
            (
                (table_ref, table),
                (states_ref, st),
                (features_ref, feat),
                (gate_in_ref, gin),
                (gate_state_ref, gst),
            )
        )
    ]
    own = [
        pltpu.make_async_copy(tout_ref, raw.at[x], own_sem.at[0]),
        pltpu.make_async_copy(tin_ref.at[pl.ds(0, 16)], win.at[y, x, z, c, 0], own_sem.at[1]),
        pltpu.make_async_copy(tin_ref.at[pl.ds(16, 16)], win.at[y, x, z, c, 1], own_sem.at[2]),
    ]
    for copy in loads + own:
        copy.start()

    entry = pltpu.get_barrier_semaphore()

    @pl.loop(1, 16)
    def _(s):
        pl.semaphore_signal(entry, 1, device_id=to_plane(lax.rem(yx + s, 16)), device_id_type=MESH)

    @pl.loop(1, 8)
    def _(s):
        pl.semaphore_signal(entry, 1, device_id=to_row(lax.rem(zc + s, 8)), device_id_type=MESH)

    firsts = (
        ("x", tout_ref, raw.at[x]),
        ("z", tin_ref.at[pl.ds(0, 16)], win.at[y, x, z, c, 0]),
        ("y", tin_ref.at[pl.ds(16, 16)], win.at[y, x, z, c, 1]),
    )
    stage1 = []
    for part, (axis, src, dst) in enumerate(firsts):
        for hop in (1, 3, 2):
            stage1.append(
                remote(
                    src,
                    send1.at[part, hop - 1],
                    recv1.at[part, hop - 1],
                    device(axis, (pos[axis] + hop) % RING),
                    dst,
                )
            )

    stage2 = []
    for part, axis in enumerate(("y", "x", "z")):
        block = (wout.at[y, z, c], win.at[y, x, :, c, 0], win.at[:, x, z, c, 1])[part]
        for hop in (1, 3, 2):
            to = device(axis, (pos[axis] + hop) % RING)
            stage2.append(remote(block, send2.at[part, hop - 1], recv2.at[part, hop - 1], to))

    def view3(part, p, h):
        if part == 0:
            return wout.at[pl.ds(2 * h, 2), p, c]
        if part == 1:
            return win.at[p, pl.ds(2 * h, 2), :, c, 0]
        return win.at[pl.ds(2 * h, 2), p, :, c, 1]

    class Ring:
        def __init__(self, view, axis, part, send, recv):
            p = pos[axis]
            up, down, far = (p + 1) % RING, (p + RING - 1) % RING, (p + 2) % RING
            right, left = device(axis, up), device(axis, down)

            def hop(n, block, h, to):
                return remote(view(part, block, h), send.at[part, n], recv.at[part, n], to)

            self.sends = [
                hop(0, p, 0, right),
                hop(1, p, 1, left),
                hop(2, p, 1, right),
                hop(3, p, 0, left),
                hop(4, down, 0, right),
                hop(5, up, 1, left),
            ]
            self.arrivals = [
                hop(0, down, 0, right),
                hop(1, up, 1, left),
                hop(2, down, 1, right),
                hop(3, up, 0, left),
                hop(4, far, 0, right),
                hop(5, far, 1, left),
            ]

        def begin(self):
            for n in range(4):
                self.sends[n].start()

        def forward(self):
            for n in (0, 1):
                self.arrivals[n].wait_recv()
                self.sends[4 + n].start()

        def arrive(self, *which):
            for n in which:
                self.arrivals[n].wait_recv()

        def drain(self):
            for copy in self.sends:
                copy.wait_send()

    pl.semaphore_wait(entry, 22)
    for copy in stage1:
        copy.start()

    both = jnp.where(
        iota((128, 512), 0) < 64,
        jnp.broadcast_to(users_ref[...].astype(F32), (128, 512)),
        jnp.broadcast_to(feats_ref[...].astype(F32), (128, 512)),
    )
    both = both.T
    user = both[:, 0:1].astype(jnp.int32)
    feature = both[:, 64:65].astype(jnp.int32)
    user_b = jnp.broadcast_to(user, (512, 128))
    lanes = iota((512, 128), 1)
    loads[0].wait()
    rows3 = jnp.zeros((512, 384), F32)
    for k in range(4):
        piece = table[pl.ds(512 * k, 512), :]
        parts = [piece & 255, (piece >> 8) & 255, piece >> 16]
        bytes3 = jnp.concatenate([v.astype(F32).astype(BF16) for v in parts], axis=1)
        pick = one_hot(iota((512, 512), 1) + 512 * k == (user >> 7))
        rows3 = rows3 + dot(pick, bytes3)
    found = rows3[:, 0:128] + 256.0 * rows3[:, 128:256] + 65536.0 * rows3[:, 256:384]
    row = jnp.sum(jnp.where(lanes == (user_b & 127), found, 0.0), axis=1, keepdims=True)
    row = row.astype(jnp.int32)
    hit = lanes == (row >> 11)
    hit16 = one_hot(hit)
    hits[...] = hit16
    before = one_hot(iota((512, 512), 1) < iota((512, 512), 0))
    rank = jnp.sum(jnp.where(hit, dot(before, hit16), 0.0), axis=1, keepdims=True)
    rank_b = jnp.broadcast_to(rank.astype(jnp.int32), (512, 128))
    ranks[...] = rank_b
    local = (row & 2047) + 1
    part = lanes // CAP
    value = jnp.where(
        part == 0,
        local & 255,
        jnp.where(part == 1, local >> 8, jnp.where(part == 2, feature & 255, feature >> 8)),
    )
    value = jnp.where((lanes % CAP == rank_b) & (part < 4), value, 0).astype(F32).astype(BF16)
    requests = dot(jnp.where(hit, 1.0, 0.0).T.astype(BF16), value)
    requests = requests + 256.0 * pltpu.roll(requests, 128 - CAP, 1)

    def spread(src, dst, mine, count, n, to):
        @pl.loop(1, count)
        def _(s):
            p = lax.rem(mine + s, count)
            remote(src(p), a2a_sem.at[n], a2a_sem.at[n + 1], to(p), dst.at[mine]).start()

    def settle(ref, count, n):
        block = ref.at[pl.ds(0, count - 1)]
        pltpu.make_async_copy(block, block, a2a_sem.at[n]).wait()

    qsend[...] = requests.reshape(16, 8, 1, 128)
    spread(lambda p: qsend.at[p], qmid, yx, 16, 0, to_plane)
    qmid[yx] = qsend[yx]

    for copy in own:
        copy.wait()
    for copy in stage1:
        copy.wait_recv()
    wout[y, z, c] = jnp.concatenate([raw[i].astype(F32) for i in range(RING)], axis=0).astype(BF16)
    for copy in stage2:
        copy.start()

    loads[1].wait()
    for k in range(4):
        st16[pl.ds(512 * k, 512), :] = st[pl.ds(512 * k, 512), :].astype(BF16)
    o = iota((512, 512), 1)
    o = (o - (o & 127)) + ((o >> 2) & 3) * 32 + ((o >> 5) & 3) * 8 + ((o >> 4) & 1) * 4 + (o & 3)
    perm[...] = one_hot(iota((512, 512), 0) == o)

    settle(qmid, 16, 1)
    spread(lambda p: qmid.at[:, p], qrecv, zc, 8, 2, to_row)
    qrecv[zc] = qmid[:, zc]

    for copy in stage2:
        copy.wait_recv()
    third = [Ring(view3, axis, part, send3, recv3) for part, axis in enumerate(("z", "y", "x"))]
    for ring in third:
        ring.begin()

    def to_sibling(part, axis, n):
        p = pos[axis]
        block = (p, (p + RING - 1) % RING, (p + 1) % RING, (p + 2) % RING)[n]
        if part == 0:
            ref = wout.at[:, block, c]
        elif part == 1:
            ref = win.at[block, :, :, c, 0]
        else:
            ref = win.at[:, block, :, c, 1]
        return remote(ref, sib_send.at[part, n], sib_recv.at[part, n], sibling)

    lasts = [[to_sibling(part, axis, n) for n in range(4)] for part, axis in enumerate(("z", "y", "x"))]
    for part in range(3):
        lasts[part][0].start()

    settle(qrecv, 8, 3)
    asked = qrecv[...].reshape(NDEV, 128)
    for k in range(CAP):
        locb[k] = jnp.broadcast_to(asked[:, k : k + 1], (NDEV, 128))
        featb[k] = jnp.broadcast_to(asked[:, 16 + k : 17 + k], (NDEV, 128))
    flipped = asked.T
    for k in range(CAP):
        locr[:, k * 128 : (k + 1) * 128] = jnp.broadcast_to(flipped[k : k + 1], (8, 128))

    def take_prior(m):
        at = locb[pl.ds(4 * m, 4)].reshape(512, 128)[:, 0:1].astype(jnp.int32)
        pick = one_hot(iota((512, 2048), 1) + 1 == at)
        prior[pl.ds(pl.multiple_of(512 * m, 512), 512), :] = dot(pick, st16[...]).astype(BF16)

    def take_inputs(m):
        at = featb[pl.ds(4 * m, 4)].reshape(512, 128)[:, 0:1].astype(jnp.int32)
        pick = one_hot(iota((512, 4096), 1) == at)
        joined[pl.ds(pl.multiple_of(512 * m, 512), 512), 512:1024] = dot(pick, feat[...]).astype(BF16)

    @pl.loop(0, 2)
    def _(m):
        take_prior(m)

    for copy in loads[2:]:
        copy.wait()
    take_inputs(0)

    for ring in third:
        ring.forward()

    take_inputs(1)

    for part in range(3):
        third[part].arrive(2, 3)
        lasts[part][1].start()
        lasts[part][2].start()

    @pl.loop(0, 4)
    def _(m):
        at = pl.ds(pl.multiple_of(256 * m, 256), 256)
        inputs = joined[at, 512:1024]
        old = prior[at, :]
        gx = dot(inputs, gin[...])
        gh = dot(old, gst[...])
        reset = 0.5 * jnp.tanh(0.5 * (gx[:, 0:512] + gh[:, 0:512])) + 0.5
        update = 0.5 * jnp.tanh(0.5 * (gx[:, 512:1024] + gh[:, 512:1024])) + 0.5
        cand = jnp.tanh(gx[:, 1024:1536] + reset * gh[:, 1024:1536])
        before = old.astype(F32)
        fresh = (1.0 - update) * cand + update * before
        joined[at, 0:512] = fresh.astype(BF16)
        dl[at, :] = (fresh - before).astype(BF16)
        xperm[at, :] = dot(inputs, perm[...]).astype(BF16)

    results = [
        pltpu.make_async_copy(dl, delta_ref, out_sem.at[0]),
        pltpu.make_async_copy(locr, slots_ref, out_sem.at[1]),
    ]
    for copy in results:
        copy.start()

    def hidden_of(a, b):
        up_y = lax.rem(y + a + a // 2 - 2 * (a // 3), RING)
        up_x = lax.rem(x + b + b // 2 - 2 * (b // 3), RING)
        at = pl.ds(pl.multiple_of(256 * (up_y * RING + up_x), 256), 256)
        v = dot_nt(joined[...], win[up_y, up_x].reshape(256, 1024))
        inner = v * (0.7978845608028654 + 0.035677408136300125 * (v * v))
        hidden[:, at] = (v + v * jnp.tanh(inner)).astype(BF16)

    for part in (1, 2):
        for n in range(3):
            lasts[part][n].wait_recv()

    @pl.loop(0, 3)
    def _(b):
        hidden_of(0, b)

    for part in (1, 2, 0):
        third[part].arrive(4, 5)
        lasts[part][3].start()

    @pl.loop(3, 9)
    def _(j):
        hidden_of(j // 3, lax.rem(j, 3))

    for part in (1, 2):
        lasts[part][3].wait_recv()

    @pl.loop(0, 7)
    def _(j):
        hidden_of(jnp.minimum(j, 3), jnp.where(j < 3, 3, j - 3))

    for copy in lasts[0]:
        copy.wait_recv()

    @pl.loop(0, 4)
    def _(m):
        at = pl.ds(pl.multiple_of(256 * m, 256), 256)
        tower = dot_nt(hidden[at, :], wout[...].reshape(512, 4096))
        prod = tower * xperm[at, :].astype(F32)
        acc[at, :] = (prod[:, 0:128] + prod[:, 128:256]) + (prod[:, 256:384] + prod[:, 384:512])

    lane = iota((NDEV, 128), 1)
    scores = jnp.zeros((NDEV, 128), F32)
    for k in range(CAP):
        s = jnp.sum(acc[k * 128 : (k + 1) * 128, :], axis=1, keepdims=True)
        scores = jnp.where(lane == k, s, scores)
    scores = scores * (0.5 / (512.0**0.5))
    ssend[...] = scores.reshape(8, 16, 1, 128)
    spread(lambda p: ssend.at[p], smid, zc, 8, 4, to_row)
    smid[zc] = ssend[zc]

    for copy in stage1:
        copy.wait_send()
    for copy in stage2:
        copy.wait_send()
    for ring in third:
        ring.drain()
    for part in range(3):
        for copy in lasts[part]:
            copy.wait_send()
    settle(qsend, 16, 0)
    settle(qrecv, 8, 2)
    settle(smid, 8, 5)
    spread(lambda p: smid.at[:, p], srecv, yx, 16, 6, to_plane)
    srecv[yx] = smid[:, yx]

    settle(srecv, 16, 7)
    back = srecv[...].reshape(NDEV, 128)
    high = back.astype(BF16)
    rest = back - high.astype(F32)
    middle = rest.astype(BF16)
    low = (rest - middle.astype(F32)).astype(BF16)
    three = jnp.concatenate([high, middle, low], axis=1)
    got = dot(hits[...], three)
    got = got[:, 0:128] + got[:, 128:256] + got[:, 256:384]
    picked = jnp.where(iota((512, 128), 1) == ranks[...], got, 0.0)
    score = jnp.sum(picked, axis=1, keepdims=True)
    score_ref[...] = jnp.broadcast_to(score, (512, 128)).T[0:1, :]
    settle(ssend, 8, 4)
    settle(srecv, 16, 6)
    for copy in results:
        copy.wait()


def update_kernel(states_ref, slots_ref, delta_ref, new_ref, st, slots, delta, in_sem, out_sem):
    parts = 4
    size = st.shape[0] // parts
    blocks = [pl.ds(size * m, size) for m in range(parts)]
    loads = [
        pltpu.make_async_copy(slots_ref, slots, in_sem.at[parts]),
        pltpu.make_async_copy(delta_ref, delta, in_sem.at[parts + 1]),
    ]
    arrivals = [
        pltpu.make_async_copy(states_ref.at[at], st.at[at], in_sem.at[m]) for m, at in enumerate(blocks)
    ]
    results = [
        pltpu.make_async_copy(st.at[at], new_ref.at[at], out_sem.at[m]) for m, at in enumerate(blocks)
    ]
    for copy in loads + arrivals:
        copy.start()
    loads[0].wait()
    owned = jnp.broadcast_to(slots[0:1, :], (size, 1024)).astype(jnp.int32)
    for m, at in enumerate(blocks):
        mine = iota((size, 1024), 0) + (size * m + 1) == owned
        count = jnp.sum(jnp.where(mine, 1.0, 0.0), axis=1, keepdims=True)
        if m == 0:
            loads[1].wait()
        total = dot(one_hot(mine), delta[...])
        arrivals[m].wait()
        st[at, :] = st[at, :] + total / jnp.maximum(count, 1.0)
        results[m].start()
    for copy in results:
        copy.wait()


def per_device(
    states,
    row_of_user,
    event_users,
    event_features,
    feature_table,
    gate_in,
    gate_state,
    tower_in,
    tower_out,
):
    table = row_of_user.reshape(2048, 128)
    anywhere = pl.BlockSpec(memory_space=pl.ANY)
    vmem = pl.BlockSpec(memory_space=pltpu.VMEM)
    dma = pltpu.SemaphoreType.DMA
    delta, slots, scores = pl.pallas_call(
        kernel,
        out_shape=(
            jax.ShapeDtypeStruct((1024, 512), BF16),
            jax.ShapeDtypeStruct((8, 1024), F32),
            jax.ShapeDtypeStruct((1, 512), F32),
        ),
        in_specs=[vmem] * 2 + [anywhere] * 7,
        out_specs=(anywhere, anywhere, vmem),
        scratch_shapes=[
            pltpu.VMEM((2048, 128), jnp.int32),
            pltpu.VMEM((2048, 512), F32),
            pltpu.VMEM((2048, 512), BF16),
            pltpu.VMEM((4096, 512), BF16),
            pltpu.VMEM((512, 1536), BF16),
            pltpu.VMEM((512, 1536), BF16),
            pltpu.VMEM((4, 4, 4, 2, 2, 16, 1024), BF16),
            pltpu.VMEM((4, 4, 2, 16, 4096), BF16),
            pltpu.VMEM((4, 4, 4096), BF16),
            pltpu.VMEM((16, 8, 1, 128), F32),
            pltpu.VMEM((16, 8, 1, 128), F32),
            pltpu.VMEM((8, 16, 1, 128), F32),
            pltpu.VMEM((8, 16, 1, 128), F32),
            pltpu.VMEM((8, 16, 1, 128), F32),
            pltpu.VMEM((16, 8, 1, 128), F32),
            pltpu.VMEM((512, 128), BF16),
            pltpu.VMEM((512, 128), jnp.int32),
            pltpu.VMEM((8, 128, 128), F32),
            pltpu.VMEM((8, 128, 128), F32),
            pltpu.VMEM((8, 1024), F32),
            pltpu.VMEM((1024, 1024), BF16),
            pltpu.VMEM((1024, 512), BF16),
            pltpu.VMEM((1024, 512), BF16),
            pltpu.VMEM((1024, 512), BF16),
            pltpu.VMEM((512, 512), BF16),
            pltpu.VMEM((1024, 4096), BF16),
            pltpu.VMEM((1024, 128), F32),
            dma((5,)),
            dma((3,)),
            dma((2,)),
            dma((8,)),
            dma((3, 3)),
            dma((3, 3)),
            dma((3, 3)),
            dma((3, 3)),
            dma((3, 6)),
            dma((3, 6)),
            dma((3, 4)),
            dma((3, 4)),
        ],
        compiler_params=pltpu.CompilerParams(
            collective_id=0, has_side_effects=True, vmem_limit_bytes=60 * 1024 * 1024
        ),
    )(event_users.reshape(1, 512), event_features.reshape(1, 512), table, states, feature_table, gate_in, gate_state, tower_in, tower_out)
    new_states = pl.pallas_call(
        update_kernel,
        out_shape=jax.ShapeDtypeStruct((2048, 512), F32),
        in_specs=[anywhere] * 3,
        out_specs=anywhere,
        scratch_shapes=[
            pltpu.VMEM((2048, 512), F32),
            pltpu.VMEM((8, 1024), F32),
            pltpu.VMEM((1024, 512), BF16),
            dma((6,)),
            dma((4,)),
        ],
        compiler_params=pltpu.CompilerParams(vmem_limit_bytes=60 * 1024 * 1024),
    )(states, slots, delta)
    return new_states, scores.reshape(512)


def solution(mesh):
    placed = (
        P(AXES, None),
        P(),
        P(AXES),
        P(AXES),
        P(),
        P(),
        P(),
        P(AXES, None),
        P(AXES, None),
    )
    return jax.shard_map(
        per_device,
        mesh=mesh,
        in_specs=placed,
        out_specs=(P(AXES, None), P(AXES)),
        check_vma=False,
    )
```

```python
import functools

import jax
import jax.numpy as jnp
from jax import lax
from jax.experimental import pallas as pl
from jax.experimental.pallas import tpu as pltpu
from jax.sharding import PartitionSpec as P

AXES = ("owner", "worker")
MESH = pl.DeviceIdType.MESH
RING = 4
NDEV = 128
CAP = 8
F32 = jnp.float32
BF16 = jnp.bfloat16


def iota(shape, dim):
    return lax.broadcasted_iota(jnp.int32, shape, dim)


def one_hot(hit):
    return jnp.where(hit, 1.0, 0.0).astype(BF16)


def dot(a, b):
    return jnp.dot(a, b, preferred_element_type=F32)


def dot_nt(a, b):
    return lax.dot_general(a, b, (((1,), (1,)), ((), ())), preferred_element_type=F32)


def kernel(
    users_ref,
    feats_ref,
    table_ref,
    states_ref,
    features_ref,
    gate_in_ref,
    gate_state_ref,
    tin_ref,
    tout_ref,
    delta_ref,
    slots_ref,
    score_ref,
    table,
    st,
    st16,
    feat,
    gin,
    gst,
    win,
    wout,
    raw,
    qsend,
    qmid,
    qrecv,
    ssend,
    smid,
    srecv,
    hits,
    ranks,
    locb,
    featb,
    locr,
    joined,
    prior,
    xperm,
    dl,
    perm,
    hidden,
    acc,
    load_sem,
    own_sem,
    out_sem,
    a2a_sem,
    send1,
    recv1,
    send2,
    recv2,
    send3,
    recv3,
    sib_send,
    sib_recv,
):
    y = lax.axis_index("owner")
    w = lax.axis_index("worker")
    x, z, c = w // 8, (w // 2) % RING, w % 2
    pos = {"x": x, "y": y, "z": z}
    yx, zc = y * RING + x, z * 2 + c

    def device(axis, p):
        at = dict(pos)
        at[axis] = p
        return (at["y"], at["x"] * 8 + at["z"] * 2 + c)

    sibling = (y, x * 8 + z * 2 + (1 - c))

    def to_plane(p):
        return (p // RING, lax.rem(p, RING) * 8 + zc)

    def to_row(p):
        return (y, x * 8 + p)

    def remote(ref, send, recv, to, dst=None):
        return pltpu.make_async_remote_copy(
            src_ref=ref,
            dst_ref=ref if dst is None else dst,
            send_sem=send,
            recv_sem=recv,
            device_id=to,
            device_id_type=MESH,
        )

    loads = [
        pltpu.make_async_copy(src, dst, load_sem.at[i])
        for i, (src, dst) in enumerate(
            (
                (table_ref, table),
                (states_ref, st),
                (features_ref, feat),
                (gate_in_ref, gin),
                (gate_state_ref, gst),
            )
        )
    ]
    own = [
        pltpu.make_async_copy(tout_ref, raw.at[x], own_sem.at[0]),
        pltpu.make_async_copy(tin_ref.at[pl.ds(0, 16)], win.at[y, x, z, c, 0], own_sem.at[1]),
        pltpu.make_async_copy(tin_ref.at[pl.ds(16, 16)], win.at[y, x, z, c, 1], own_sem.at[2]),
    ]
    for copy in loads + own:
        copy.start()

    entry = pltpu.get_barrier_semaphore()

    @pl.loop(1, 16)
    def _(s):
        pl.semaphore_signal(entry, 1, device_id=to_plane(lax.rem(yx + s, 16)), device_id_type=MESH)

    @pl.loop(1, 8)
    def _(s):
        pl.semaphore_signal(entry, 1, device_id=to_row(lax.rem(zc + s, 8)), device_id_type=MESH)

    firsts = (
        ("x", tout_ref, raw.at[x]),
        ("z", tin_ref.at[pl.ds(0, 16)], win.at[y, x, z, c, 0]),
        ("y", tin_ref.at[pl.ds(16, 16)], win.at[y, x, z, c, 1]),
    )
    stage1 = []
    for part, (axis, src, dst) in enumerate(firsts):
        for hop in (1, 3, 2):
            stage1.append(
                remote(
                    src,
                    send1.at[part, hop - 1],
                    recv1.at[part, hop - 1],
                    device(axis, (pos[axis] + hop) % RING),
                    dst,
                )
            )

    stage2 = []
    for part, axis in enumerate(("y", "x", "z")):
        block = (wout.at[y, z, c], win.at[y, x, :, c, 0], win.at[:, x, z, c, 1])[part]
        for hop in (1, 3, 2):
            to = device(axis, (pos[axis] + hop) % RING)
            stage2.append(remote(block, send2.at[part, hop - 1], recv2.at[part, hop - 1], to))

    def view3(part, p, h):
        if part == 0:
            return wout.at[pl.ds(2 * h, 2), p, c]
        if part == 1:
            return win.at[p, pl.ds(2 * h, 2), :, c, 0]
        return win.at[pl.ds(2 * h, 2), p, :, c, 1]

    class Ring:
        def __init__(self, view, axis, part, send, recv):
            p = pos[axis]
            up, down, far = (p + 1) % RING, (p + RING - 1) % RING, (p + 2) % RING
            right, left = device(axis, up), device(axis, down)

            def hop(n, block, h, to):
                return remote(view(part, block, h), send.at[part, n], recv.at[part, n], to)

            self.sends = [
                hop(0, p, 0, right),
                hop(1, p, 1, left),
                hop(2, p, 1, right),
                hop(3, p, 0, left),
                hop(4, down, 0, right),
                hop(5, up, 1, left),
            ]
            self.arrivals = [
                hop(0, down, 0, right),
                hop(1, up, 1, left),
                hop(2, down, 1, right),
                hop(3, up, 0, left),
                hop(4, far, 0, right),
                hop(5, far, 1, left),
            ]

        def begin(self):
            for n in range(4):
                self.sends[n].start()

        def forward(self):
            for n in (0, 1):
                self.arrivals[n].wait_recv()
                self.sends[4 + n].start()

        def arrive(self, *which):
            for n in which:
                self.arrivals[n].wait_recv()

        def drain(self):
            for copy in self.sends:
                copy.wait_send()

    pl.semaphore_wait(entry, 22)
    for copy in stage1:
        copy.start()

    both = jnp.where(
        iota((128, 512), 0) < 64,
        jnp.broadcast_to(users_ref[...].astype(F32), (128, 512)),
        jnp.broadcast_to(feats_ref[...].astype(F32), (128, 512)),
    )
    both = both.T
    user = both[:, 0:1].astype(jnp.int32)
    feature = both[:, 64:65].astype(jnp.int32)
    user_b = jnp.broadcast_to(user, (512, 128))
    lanes = iota((512, 128), 1)
    loads[0].wait()
    rows3 = jnp.zeros((512, 384), F32)
    for k in range(4):
        piece = table[pl.ds(512 * k, 512), :]
        parts = [piece & 255, (piece >> 8) & 255, piece >> 16]
        bytes3 = jnp.concatenate([v.astype(F32).astype(BF16) for v in parts], axis=1)
        pick = one_hot(iota((512, 512), 1) + 512 * k == (user >> 7))
        rows3 = rows3 + dot(pick, bytes3)
    found = rows3[:, 0:128] + 256.0 * rows3[:, 128:256] + 65536.0 * rows3[:, 256:384]
    row = jnp.sum(jnp.where(lanes == (user_b & 127), found, 0.0), axis=1, keepdims=True)
    row = row.astype(jnp.int32)
    hit = lanes == (row >> 11)
    hit16 = one_hot(hit)
    hits[...] = hit16
    before = one_hot(iota((512, 512), 1) < iota((512, 512), 0))
    rank = jnp.sum(jnp.where(hit, dot(before, hit16), 0.0), axis=1, keepdims=True)
    rank_b = jnp.broadcast_to(rank.astype(jnp.int32), (512, 128))
    ranks[...] = rank_b
    local = (row & 2047) + 1
    part = lanes // CAP
    value = jnp.where(
        part == 0,
        local & 255,
        jnp.where(part == 1, local >> 8, jnp.where(part == 2, feature & 255, feature >> 8)),
    )
    value = jnp.where((lanes % CAP == rank_b) & (part < 4), value, 0).astype(F32).astype(BF16)
    requests = dot(jnp.where(hit, 1.0, 0.0).T.astype(BF16), value)
    requests = requests + 256.0 * pltpu.roll(requests, 128 - CAP, 1)

    def spread(src, dst, mine, count, n, to):
        @pl.loop(1, count, unroll=True)
        def _(s):
            p = lax.rem(mine + s, count)
            remote(src(p), a2a_sem.at[n], a2a_sem.at[n + 1], to(p), dst.at[mine]).start()

    def settle(ref, count, n):
        block = ref.at[pl.ds(0, count - 1)]
        pltpu.make_async_copy(block, block, a2a_sem.at[n]).wait()

    qsend[...] = requests.reshape(16, 8, 1, 128)
    spread(lambda p: qsend.at[p], qmid, yx, 16, 0, to_plane)
    qmid[yx] = qsend[yx]

    for copy in own:
        copy.wait()
    for copy in stage1:
        copy.wait_recv()
    mine = jnp.concatenate([raw[i].astype(F32) for i in range(RING)], axis=0).astype(BF16)
    j = iota((256, 256), 1)
    order = one_hot(iota((256, 256), 0) == ((j & 127) >> 4) * 32 + (j >> 7) * 16 + (j & 15))
    for g in range(16):
        wout[y, z, c, :, 256 * g : 256 * (g + 1)] = dot(mine[:, 256 * g : 256 * (g + 1)], order).astype(BF16)
    for copy in stage2:
        copy.start()

    loads[1].wait()
    for k in range(4):
        st16[pl.ds(512 * k, 512), :] = st[pl.ds(512 * k, 512), :].astype(BF16)
    o = iota((512, 512), 1)
    o = (o - (o & 127)) + ((o >> 2) & 3) * 32 + ((o >> 5) & 3) * 8 + ((o >> 4) & 1) * 4 + (o & 3)
    perm[...] = one_hot(iota((512, 512), 0) == o)

    settle(qmid, 16, 1)
    spread(lambda p: qmid.at[:, p], qrecv, zc, 8, 2, to_row)
    qrecv[zc] = qmid[:, zc]

    for copy in stage2:
        copy.wait_recv()
    third = [Ring(view3, axis, part, send3, recv3) for part, axis in enumerate(("z", "y", "x"))]
    for ring in third:
        ring.begin()

    def to_sibling(part, axis, n):
        p = pos[axis]
        block = (p, (p + RING - 1) % RING, (p + 1) % RING, (p + 2) % RING)[n]
        if part == 0:
            ref = wout.at[:, block, c]
        elif part == 1:
            ref = win.at[block, :, :, c, 0]
        else:
            ref = win.at[:, block, :, c, 1]
        return remote(ref, sib_send.at[part, n], sib_recv.at[part, n], sibling)

    lasts = [[to_sibling(part, axis, n) for n in range(4)] for part, axis in enumerate(("z", "y", "x"))]
    for part in range(3):
        lasts[part][0].start()

    settle(qrecv, 8, 3)
    asked = qrecv[...].reshape(NDEV, 128)
    for k in range(CAP):
        locb[k] = jnp.broadcast_to(asked[:, k : k + 1], (NDEV, 128))
        featb[k] = jnp.broadcast_to(asked[:, 16 + k : 17 + k], (NDEV, 128))
    flipped = asked.T
    for k in range(CAP):
        locr[:, k * 128 : (k + 1) * 128] = jnp.broadcast_to(flipped[k : k + 1], (8, 128))

    def take_prior(m):
        at = locb[pl.ds(4 * m, 4)].reshape(512, 128)[:, 0:1].astype(jnp.int32)
        pick = one_hot(iota((512, 2048), 1) + 1 == at)
        prior[pl.ds(pl.multiple_of(512 * m, 512), 512), :] = dot(pick, st16[...]).astype(BF16)

    def take_inputs(m):
        at = featb[pl.ds(4 * m, 4)].reshape(512, 128)[:, 0:1].astype(jnp.int32)
        pick = one_hot(iota((512, 4096), 1) == at)
        joined[pl.ds(pl.multiple_of(512 * m, 512), 512), 512:1024] = dot(pick, feat[...]).astype(BF16)

    @pl.loop(0, 2)
    def _(m):
        take_prior(m)

    for copy in loads[2:]:
        copy.wait()
    take_inputs(0)

    for ring in third:
        ring.forward()

    take_inputs(1)

    for part in range(3):
        third[part].arrive(2, 3)
        lasts[part][1].start()
        lasts[part][2].start()

    @pl.loop(0, 4)
    def _(m):
        at = pl.ds(pl.multiple_of(256 * m, 256), 256)
        inputs = joined[at, 512:1024]
        old = prior[at, :]
        gx = dot(inputs, gin[...])
        gh = dot(old, gst[...])
        reset = 0.5 * jnp.tanh(0.5 * (gx[:, 0:512] + gh[:, 0:512])) + 0.5
        update = 0.5 * jnp.tanh(0.5 * (gx[:, 512:1024] + gh[:, 512:1024])) + 0.5
        cand = jnp.tanh(gx[:, 1024:1536] + reset * gh[:, 1024:1536])
        before = old.astype(F32)
        fresh = (1.0 - update) * cand + update * before
        joined[at, 0:512] = fresh.astype(BF16)
        dl[at, :] = (fresh - before).astype(BF16)
        xperm[at, :] = dot(inputs, perm[...]).astype(BF16)

    results = [
        pltpu.make_async_copy(dl, delta_ref, out_sem.at[0]),
        pltpu.make_async_copy(locr, slots_ref, out_sem.at[1]),
    ]
    for copy in results:
        copy.start()

    def activate(weights, store):
        for m in range(2):
            at = pl.ds(512 * m, 512)
            v = dot_nt(joined[at, :], weights())
            inner = v * (0.7978845608028654 + 0.035677408136300125 * (v * v))
            done = (v + v * jnp.tanh(inner)).astype(BF16)
            for i in range(RING):
                hidden[at, pl.ds(pl.multiple_of(store(i), 128), 128)] = done[:, 128 * i : 128 * (i + 1)]

    def unit(hop):
        p = lax.rem(y + hop, RING)
        q = lax.rem(x + hop, RING)
        activate(lambda: win[p, :, :, :, 0].reshape(512, 1024), lambda i: 1024 * p + 256 * i)
        activate(lambda: win[:, q, :, :, 1].reshape(512, 1024), lambda i: 1024 * i + 256 * q + 128)

    for part in (1, 2):
        lasts[part][0].wait_recv()
    unit(0)

    for part in (1, 2, 0):
        third[part].arrive(4, 5)
        lasts[part][3].start()
    for part in (1, 2):
        for n in (1, 2):
            lasts[part][n].wait_recv()

    @pl.loop(0, 2)
    def _(j):
        unit(1 + 2 * j)

    for part in (1, 2):
        lasts[part][3].wait_recv()
    unit(2)

    for copy in lasts[0]:
        copy.wait_recv()

    for m in range(2):
        at = pl.ds(512 * m, 512)
        tower = dot_nt(hidden[at, :], wout[...].reshape(512, 4096))
        prod = tower * xperm[at, :].astype(F32)
        acc[at, :] = (prod[:, 0:128] + prod[:, 128:256]) + (prod[:, 256:384] + prod[:, 384:512])

    lane = iota((NDEV, 128), 1)
    scores = jnp.zeros((NDEV, 128), F32)
    for k in range(CAP):
        s = jnp.sum(acc[k * 128 : (k + 1) * 128, :], axis=1, keepdims=True)
        scores = jnp.where(lane == k, s, scores)
    scores = scores * (0.5 / (512.0**0.5))
    ssend[...] = scores.reshape(8, 16, 1, 128)
    spread(lambda p: ssend.at[p], smid, zc, 8, 4, to_row)
    smid[zc] = ssend[zc]

    for copy in stage1:
        copy.wait_send()
    for copy in stage2:
        copy.wait_send()
    for ring in third:
        ring.drain()
    for part in range(3):
        for copy in lasts[part]:
            copy.wait_send()
    settle(qsend, 16, 0)
    settle(qrecv, 8, 2)
    settle(smid, 8, 5)
    spread(lambda p: smid.at[:, p], srecv, yx, 16, 6, to_plane)
    srecv[yx] = smid[:, yx]

    settle(srecv, 16, 7)
    back = srecv[...].reshape(NDEV, 128)
    high = back.astype(BF16)
    rest = back - high.astype(F32)
    middle = rest.astype(BF16)
    low = (rest - middle.astype(F32)).astype(BF16)
    three = jnp.concatenate([high, middle, low], axis=1)
    got = dot(hits[...], three)
    got = got[:, 0:128] + got[:, 128:256] + got[:, 256:384]
    picked = jnp.where(iota((512, 128), 1) == ranks[...], got, 0.0)
    score = jnp.sum(picked, axis=1, keepdims=True)
    score_ref[...] = jnp.broadcast_to(score, (512, 128)).T[0:1, :]
    settle(ssend, 8, 4)
    settle(srecv, 16, 6)
    for copy in results:
        copy.wait()


def update_kernel(states_ref, slots_ref, delta_ref, new_ref, st, slots, delta, in_sem, out_sem):
    parts = 4
    size = st.shape[0] // parts
    blocks = [pl.ds(size * m, size) for m in range(parts)]
    loads = [
        pltpu.make_async_copy(slots_ref, slots, in_sem.at[parts]),
        pltpu.make_async_copy(delta_ref, delta, in_sem.at[parts + 1]),
    ]
    arrivals = [
        pltpu.make_async_copy(states_ref.at[at], st.at[at], in_sem.at[m]) for m, at in enumerate(blocks)
    ]
    results = [
        pltpu.make_async_copy(st.at[at], new_ref.at[at], out_sem.at[m]) for m, at in enumerate(blocks)
    ]
    for copy in loads + arrivals:
        copy.start()
    loads[0].wait()
    owned = jnp.broadcast_to(slots[0:1, :], (size, 1024)).astype(jnp.int32)
    for m, at in enumerate(blocks):
        mine = iota((size, 1024), 0) + (size * m + 1) == owned
        count = jnp.sum(jnp.where(mine, 1.0, 0.0), axis=1, keepdims=True)
        if m == 0:
            loads[1].wait()
        total = dot(one_hot(mine), delta[...])
        arrivals[m].wait()
        st[at, :] = st[at, :] + total / jnp.maximum(count, 1.0)
        results[m].start()
    for copy in results:
        copy.wait()


def per_device(
    states,
    row_of_user,
    event_users,
    event_features,
    feature_table,
    gate_in,
    gate_state,
    tower_in,
    tower_out,
):
    table = row_of_user.reshape(2048, 128)
    anywhere = pl.BlockSpec(memory_space=pl.ANY)
    vmem = pl.BlockSpec(memory_space=pltpu.VMEM)
    dma = pltpu.SemaphoreType.DMA
    delta, slots, scores = pl.pallas_call(
        kernel,
        out_shape=(
            jax.ShapeDtypeStruct((1024, 512), BF16),
            jax.ShapeDtypeStruct((8, 1024), F32),
            jax.ShapeDtypeStruct((1, 512), F32),
        ),
        in_specs=[vmem] * 2 + [anywhere] * 7,
        out_specs=(anywhere, anywhere, vmem),
        scratch_shapes=[
            pltpu.VMEM((2048, 128), jnp.int32),
            pltpu.VMEM((2048, 512), F32),
            pltpu.VMEM((2048, 512), BF16),
            pltpu.VMEM((4096, 512), BF16),
            pltpu.VMEM((512, 1536), BF16),
            pltpu.VMEM((512, 1536), BF16),
            pltpu.VMEM((4, 4, 4, 2, 2, 16, 1024), BF16),
            pltpu.VMEM((4, 4, 2, 16, 4096), BF16),
            pltpu.VMEM((4, 4, 4096), BF16),
            pltpu.VMEM((16, 8, 1, 128), F32),
            pltpu.VMEM((16, 8, 1, 128), F32),
            pltpu.VMEM((8, 16, 1, 128), F32),
            pltpu.VMEM((8, 16, 1, 128), F32),
            pltpu.VMEM((8, 16, 1, 128), F32),
            pltpu.VMEM((16, 8, 1, 128), F32),
            pltpu.VMEM((512, 128), BF16),
            pltpu.VMEM((512, 128), jnp.int32),
            pltpu.VMEM((8, 128, 128), F32),
            pltpu.VMEM((8, 128, 128), F32),
            pltpu.VMEM((8, 1024), F32),
            pltpu.VMEM((1024, 1024), BF16),
            pltpu.VMEM((1024, 512), BF16),
            pltpu.VMEM((1024, 512), BF16),
            pltpu.VMEM((1024, 512), BF16),
            pltpu.VMEM((512, 512), BF16),
            pltpu.VMEM((1024, 4096), BF16),
            pltpu.VMEM((1024, 128), F32),
            dma((5,)),
            dma((3,)),
            dma((2,)),
            dma((8,)),
            dma((3, 3)),
            dma((3, 3)),
            dma((3, 3)),
            dma((3, 3)),
            dma((3, 6)),
            dma((3, 6)),
            dma((3, 4)),
            dma((3, 4)),
        ],
        compiler_params=pltpu.CompilerParams(
            collective_id=0, has_side_effects=True, vmem_limit_bytes=60 * 1024 * 1024
        ),
    )(event_users.reshape(1, 512), event_features.reshape(1, 512), table, states, feature_table, gate_in, gate_state, tower_in, tower_out)
    new_states = pl.pallas_call(
        update_kernel,
        out_shape=jax.ShapeDtypeStruct((2048, 512), F32),
        in_specs=[anywhere] * 3,
        out_specs=anywhere,
        scratch_shapes=[
            pltpu.VMEM((2048, 512), F32),
            pltpu.VMEM((8, 1024), F32),
            pltpu.VMEM((1024, 512), BF16),
            dma((6,)),
            dma((4,)),
        ],
        compiler_params=pltpu.CompilerParams(vmem_limit_bytes=60 * 1024 * 1024),
    )(states, slots, delta)
    return new_states, scores.reshape(512)


def solution(mesh):
    placed = (
        P(AXES, None),
        P(),
        P(AXES),
        P(AXES),
        P(),
        P(),
        P(),
        P(AXES, None),
        P(AXES, None),
    )
    return jax.shard_map(
        per_device,
        mesh=mesh,
        in_specs=placed,
        out_specs=(P(AXES, None), P(AXES)),
        check_vma=False,
    )
```

```python
import functools

import jax
import jax.numpy as jnp
from jax import lax
from jax.experimental import pallas as pl
from jax.experimental.pallas import tpu as pltpu
from jax.sharding import PartitionSpec as P

AXES = ("owner", "worker")
MESH = pl.DeviceIdType.MESH
RING = 4
NDEV = 128
CAP = 8
F32 = jnp.float32
BF16 = jnp.bfloat16


def iota(shape, dim):
    return lax.broadcasted_iota(jnp.int32, shape, dim)


def one_hot(hit):
    return jnp.where(hit, 1.0, 0.0).astype(BF16)


def dot(a, b):
    return jnp.dot(a, b, preferred_element_type=F32)


def dot_nt(a, b):
    return lax.dot_general(a, b, (((1,), (1,)), ((), ())), preferred_element_type=F32)


def kernel(
    users_ref,
    feats_ref,
    table_ref,
    states_ref,
    features_ref,
    gate_in_ref,
    gate_state_ref,
    tin_ref,
    tout_ref,
    mean_ref,
    score_ref,
    table,
    st,
    st16,
    feat,
    gin,
    gst,
    win,
    wout,
    raw,
    qsend,
    qmid,
    qrecv,
    ssend,
    smid,
    srecv,
    hits,
    ranks,
    locb,
    featb,
    locr,
    joined,
    prior,
    xperm,
    dl,
    perm,
    hidden,
    means,
    acc,
    load_sem,
    own_sem,
    out_sem,
    a2a_sem,
    send1,
    recv1,
    send2,
    recv2,
    send3,
    recv3,
    sib_send,
    sib_recv,
):
    y = lax.axis_index("owner")
    w = lax.axis_index("worker")
    x, z, c = w // 8, (w // 2) % RING, w % 2
    pos = {"x": x, "y": y, "z": z}
    yx, zc = y * RING + x, z * 2 + c

    def device(axis, p):
        at = dict(pos)
        at[axis] = p
        return (at["y"], at["x"] * 8 + at["z"] * 2 + c)

    sibling = (y, x * 8 + z * 2 + (1 - c))

    def to_plane(p):
        return (p // RING, lax.rem(p, RING) * 8 + zc)

    def to_row(p):
        return (y, x * 8 + p)

    def remote(ref, send, recv, to, dst=None):
        return pltpu.make_async_remote_copy(
            src_ref=ref,
            dst_ref=ref if dst is None else dst,
            send_sem=send,
            recv_sem=recv,
            device_id=to,
            device_id_type=MESH,
        )

    loads = [
        pltpu.make_async_copy(src, dst, load_sem.at[i])
        for i, (src, dst) in enumerate(
            (
                (table_ref, table),
                (states_ref, st),
                (features_ref, feat),
                (gate_in_ref, gin),
                (gate_state_ref, gst),
            )
        )
    ]
    own = [
        pltpu.make_async_copy(tout_ref, raw.at[x], own_sem.at[0]),
        pltpu.make_async_copy(tin_ref.at[pl.ds(0, 16)], win.at[y, x, z, c, 0], own_sem.at[1]),
        pltpu.make_async_copy(tin_ref.at[pl.ds(16, 16)], win.at[y, x, z, c, 1], own_sem.at[2]),
    ]
    for copy in loads + own:
        copy.start()

    entry = pltpu.get_barrier_semaphore()

    @pl.loop(1, 16)
    def _(s):
        pl.semaphore_signal(entry, 1, device_id=to_plane(lax.rem(yx + s, 16)), device_id_type=MESH)

    @pl.loop(1, 8)
    def _(s):
        pl.semaphore_signal(entry, 1, device_id=to_row(lax.rem(zc + s, 8)), device_id_type=MESH)

    firsts = (
        ("x", tout_ref, raw.at[x]),
        ("z", tin_ref.at[pl.ds(0, 16)], win.at[y, x, z, c, 0]),
        ("y", tin_ref.at[pl.ds(16, 16)], win.at[y, x, z, c, 1]),
    )
    stage1 = []
    for part, (axis, src, dst) in enumerate(firsts):
        for hop in (1, 3, 2):
            stage1.append(
                remote(
                    src,
                    send1.at[part, hop - 1],
                    recv1.at[part, hop - 1],
                    device(axis, (pos[axis] + hop) % RING),
                    dst,
                )
            )

    stage2 = []
    for part, axis in enumerate(("y", "x", "z")):
        block = (wout.at[y, z, c], win.at[y, x, :, c, 0], win.at[:, x, z, c, 1])[part]
        for hop in (1, 3, 2):
            to = device(axis, (pos[axis] + hop) % RING)
            stage2.append(remote(block, send2.at[part, hop - 1], recv2.at[part, hop - 1], to))

    def view3(part, p, h):
        if part == 0:
            return wout.at[pl.ds(2 * h, 2), p, c]
        if part == 1:
            return win.at[p, pl.ds(2 * h, 2), :, c, 0]
        return win.at[pl.ds(2 * h, 2), p, :, c, 1]

    class Ring:
        def __init__(self, view, axis, part, send, recv):
            p = pos[axis]
            up, down, far = (p + 1) % RING, (p + RING - 1) % RING, (p + 2) % RING
            right, left = device(axis, up), device(axis, down)

            def hop(n, block, h, to):
                return remote(view(part, block, h), send.at[part, n], recv.at[part, n], to)

            self.sends = [
                hop(0, p, 0, right),
                hop(1, p, 1, left),
                hop(2, p, 1, right),
                hop(3, p, 0, left),
                hop(4, down, 0, right),
                hop(5, up, 1, left),
            ]
            self.arrivals = [
                hop(0, down, 0, right),
                hop(1, up, 1, left),
                hop(2, down, 1, right),
                hop(3, up, 0, left),
                hop(4, far, 0, right),
                hop(5, far, 1, left),
            ]

        def begin(self):
            for n in range(4):
                self.sends[n].start()

        def forward(self):
            for n in (0, 1):
                self.arrivals[n].wait_recv()
                self.sends[4 + n].start()

        def arrive(self, *which):
            for n in which:
                self.arrivals[n].wait_recv()

        def drain(self):
            for copy in self.sends:
                copy.wait_send()

    pl.semaphore_wait(entry, 22)
    for copy in stage1:
        copy.start()

    both = jnp.where(
        iota((128, 512), 0) < 64,
        jnp.broadcast_to(users_ref[...].astype(F32), (128, 512)),
        jnp.broadcast_to(feats_ref[...].astype(F32), (128, 512)),
    )
    both = both.T
    user = both[:, 0:1].astype(jnp.int32)
    feature = both[:, 64:65].astype(jnp.int32)
    user_b = jnp.broadcast_to(user, (512, 128))
    lanes = iota((512, 128), 1)
    loads[0].wait()
    rows3 = jnp.zeros((512, 384), F32)
    for k in range(4):
        piece = table[pl.ds(512 * k, 512), :]
        parts = [piece & 255, (piece >> 8) & 255, piece >> 16]
        bytes3 = jnp.concatenate([v.astype(F32).astype(BF16) for v in parts], axis=1)
        pick = one_hot(iota((512, 512), 1) + 512 * k == (user >> 7))
        rows3 = rows3 + dot(pick, bytes3)
    found = rows3[:, 0:128] + 256.0 * rows3[:, 128:256] + 65536.0 * rows3[:, 256:384]
    row = jnp.sum(jnp.where(lanes == (user_b & 127), found, 0.0), axis=1, keepdims=True)
    row = row.astype(jnp.int32)
    hit = lanes == (row >> 11)
    hit16 = one_hot(hit)
    hits[...] = hit16
    before = one_hot(iota((512, 512), 1) < iota((512, 512), 0))
    rank = jnp.sum(jnp.where(hit, dot(before, hit16), 0.0), axis=1, keepdims=True)
    rank_b = jnp.broadcast_to(rank.astype(jnp.int32), (512, 128))
    ranks[...] = rank_b
    local = (row & 2047) + 1
    part = lanes // CAP
    value = jnp.where(
        part == 0,
        local & 255,
        jnp.where(part == 1, local >> 8, jnp.where(part == 2, feature & 255, feature >> 8)),
    )
    value = jnp.where((lanes % CAP == rank_b) & (part < 4), value, 0).astype(F32).astype(BF16)
    requests = dot(jnp.where(hit, 1.0, 0.0).T.astype(BF16), value)
    requests = requests + 256.0 * pltpu.roll(requests, 128 - CAP, 1)

    def spread(src, dst, mine, count, n, to):
        @pl.loop(1, count, unroll=True)
        def _(s):
            p = lax.rem(mine + s, count)
            remote(src(p), a2a_sem.at[n], a2a_sem.at[n + 1], to(p), dst.at[mine]).start()

    def settle(ref, count, n):
        block = ref.at[pl.ds(0, count - 1)]
        pltpu.make_async_copy(block, block, a2a_sem.at[n]).wait()

    qsend[...] = requests.reshape(16, 8, 1, 128)
    spread(lambda p: qsend.at[p], qmid, yx, 16, 0, to_plane)
    qmid[yx] = qsend[yx]

    for copy in own:
        copy.wait()
    for copy in stage1:
        copy.wait_recv()
    mine = jnp.concatenate([raw[i].astype(F32) for i in range(RING)], axis=0).astype(BF16)
    j = iota((256, 256), 1)
    order = one_hot(iota((256, 256), 0) == ((j & 127) >> 4) * 32 + (j >> 7) * 16 + (j & 15))
    for g in range(16):
        wout[y, z, c, :, 256 * g : 256 * (g + 1)] = dot(mine[:, 256 * g : 256 * (g + 1)], order).astype(BF16)
    for copy in stage2:
        copy.start()

    loads[1].wait()
    for k in range(4):
        st16[pl.ds(512 * k, 512), :] = st[pl.ds(512 * k, 512), :].astype(BF16)
    o = iota((512, 512), 1)
    o = (o - (o & 127)) + ((o >> 2) & 3) * 32 + ((o >> 5) & 3) * 8 + ((o >> 4) & 1) * 4 + (o & 3)
    perm[...] = one_hot(iota((512, 512), 0) == o)

    settle(qmid, 16, 1)
    spread(lambda p: qmid.at[:, p], qrecv, zc, 8, 2, to_row)
    qrecv[zc] = qmid[:, zc]

    for copy in stage2:
        copy.wait_recv()
    third = [Ring(view3, axis, part, send3, recv3) for part, axis in enumerate(("z", "y", "x"))]
    for ring in third:
        ring.begin()

    def to_sibling(part, axis, n):
        p = pos[axis]
        block = (p, (p + RING - 1) % RING, (p + 1) % RING, (p + 2) % RING)[n]
        if part == 0:
            ref = wout.at[:, block, c]
        elif part == 1:
            ref = win.at[block, :, :, c, 0]
        else:
            ref = win.at[:, block, :, c, 1]
        return remote(ref, sib_send.at[part, n], sib_recv.at[part, n], sibling)

    lasts = [[to_sibling(part, axis, n) for n in range(4)] for part, axis in enumerate(("z", "y", "x"))]
    for part in range(3):
        lasts[part][0].start()

    settle(qrecv, 8, 3)
    asked = qrecv[...].reshape(NDEV, 128)
    for k in range(CAP):
        locb[k] = jnp.broadcast_to(asked[:, k : k + 1], (NDEV, 128))
        featb[k] = jnp.broadcast_to(asked[:, 16 + k : 17 + k], (NDEV, 128))
    flipped = asked.T
    for k in range(CAP):
        locr[:, k * 128 : (k + 1) * 128] = jnp.broadcast_to(flipped[k : k + 1], (8, 128))

    def take_prior(m):
        at = locb[pl.ds(4 * m, 4)].reshape(512, 128)[:, 0:1].astype(jnp.int32)
        pick = one_hot(iota((512, 2048), 1) + 1 == at)
        prior[pl.ds(pl.multiple_of(512 * m, 512), 512), :] = dot(pick, st16[...]).astype(BF16)

    def take_inputs(m):
        at = featb[pl.ds(4 * m, 4)].reshape(512, 128)[:, 0:1].astype(jnp.int32)
        pick = one_hot(iota((512, 4096), 1) == at)
        joined[pl.ds(pl.multiple_of(512 * m, 512), 512), 512:1024] = dot(pick, feat[...]).astype(BF16)

    @pl.loop(0, 2)
    def _(m):
        take_prior(m)

    for copy in loads[2:]:
        copy.wait()
    take_inputs(0)

    for ring in third:
        ring.forward()

    take_inputs(1)

    for part in range(3):
        third[part].arrive(2, 3)
        lasts[part][1].start()
        lasts[part][2].start()

    @pl.loop(0, 4)
    def _(m):
        at = pl.ds(pl.multiple_of(256 * m, 256), 256)
        inputs = joined[at, 512:1024]
        old = prior[at, :]
        gx = dot(inputs, gin[...])
        gh = dot(old, gst[...])
        reset = 0.5 * jnp.tanh(0.5 * (gx[:, 0:512] + gh[:, 0:512])) + 0.5
        update = 0.5 * jnp.tanh(0.5 * (gx[:, 512:1024] + gh[:, 512:1024])) + 0.5
        cand = jnp.tanh(gx[:, 1024:1536] + reset * gh[:, 1024:1536])
        before = old.astype(F32)
        fresh = (1.0 - update) * cand + update * before
        joined[at, 0:512] = fresh.astype(BF16)
        dl[at, :] = (fresh - before).astype(BF16)
        xperm[at, :] = dot(inputs, perm[...]).astype(BF16)


    def activate(weights, store):
        for m in range(2):
            at = pl.ds(512 * m, 512)
            v = dot_nt(joined[at, :], weights())
            inner = v * (0.7978845608028654 + 0.035677408136300125 * (v * v))
            done = (v + v * jnp.tanh(inner)).astype(BF16)
            for i in range(RING):
                hidden[at, pl.ds(pl.multiple_of(store(i), 128), 128)] = done[:, 128 * i : 128 * (i + 1)]

    def unit(hop):
        p = lax.rem(y + hop, RING)
        q = lax.rem(x + hop, RING)
        activate(lambda: win[p, :, :, :, 0].reshape(512, 1024), lambda i: 1024 * p + 256 * i)
        activate(lambda: win[:, q, :, :, 1].reshape(512, 1024), lambda i: 1024 * i + 256 * q + 128)

    for part in (1, 2):
        lasts[part][0].wait_recv()
    unit(0)

    for part in (1, 2, 0):
        third[part].arrive(4, 5)
        lasts[part][3].start()
    for part in (1, 2):
        for n in (1, 2):
            lasts[part][n].wait_recv()

    @pl.loop(0, 2)
    def _(j):
        unit(1 + 2 * j)

    for part in (1, 2):
        lasts[part][3].wait_recv()
    unit(2)

    for copy in lasts[0]:
        copy.wait_recv()

    for m in range(2):
        at = pl.ds(512 * m, 512)
        tower = dot_nt(hidden[at, :], wout[...].reshape(512, 4096))
        prod = tower * xperm[at, :].astype(F32)
        acc[at, :] = (prod[:, 0:128] + prod[:, 128:256]) + (prod[:, 256:384] + prod[:, 384:512])

    lane = iota((NDEV, 128), 1)
    scores = jnp.zeros((NDEV, 128), F32)
    for k in range(CAP):
        s = jnp.sum(acc[k * 128 : (k + 1) * 128, :], axis=1, keepdims=True)
        scores = jnp.where(lane == k, s, scores)
    scores = scores * (0.5 / (512.0**0.5))
    ssend[...] = scores.reshape(8, 16, 1, 128)
    spread(lambda p: ssend.at[p], smid, zc, 8, 4, to_row)
    smid[zc] = ssend[zc]

    owned = jnp.broadcast_to(locr[0:1, :], (512, 1024)).astype(jnp.int32)
    results = []

    def mean_of(m):
        at = pl.ds(512 * m, 512)
        matches = iota((512, 1024), 0) + (512 * m + 1) == owned
        count = jnp.sum(jnp.where(matches, 1.0, 0.0), axis=1, keepdims=True)
        means[at, :] = (dot(one_hot(matches), dl[...]) / jnp.maximum(count, 1.0)).astype(BF16)
        results.append(pltpu.make_async_copy(means.at[at], mean_ref.at[at], out_sem.at[m]))
        results[m].start()

    mean_of(0)
    mean_of(1)

    for copy in stage1:
        copy.wait_send()
    for copy in stage2:
        copy.wait_send()
    for ring in third:
        ring.drain()
    for part in range(3):
        for copy in lasts[part]:
            copy.wait_send()
    settle(qsend, 16, 0)
    settle(qrecv, 8, 2)
    settle(smid, 8, 5)
    spread(lambda p: smid.at[:, p], srecv, yx, 16, 6, to_plane)
    srecv[yx] = smid[:, yx]
    mean_of(2)
    mean_of(3)

    settle(srecv, 16, 7)
    back = srecv[...].reshape(NDEV, 128)
    high = back.astype(BF16)
    rest = back - high.astype(F32)
    middle = rest.astype(BF16)
    low = (rest - middle.astype(F32)).astype(BF16)
    three = jnp.concatenate([high, middle, low], axis=1)
    got = dot(hits[...], three)
    got = got[:, 0:128] + got[:, 128:256] + got[:, 256:384]
    picked = jnp.where(iota((512, 128), 1) == ranks[...], got, 0.0)
    score = jnp.sum(picked, axis=1, keepdims=True)
    score_ref[...] = jnp.broadcast_to(score, (512, 128)).T[0:1, :]
    settle(ssend, 8, 4)
    settle(srecv, 16, 6)
    for copy in results:
        copy.wait()


def update_kernel(states_ref, mean_ref, new_ref, st, mean, in_sem, mean_sem, out_sem):
    parts = 8
    size = st.shape[0] // parts
    blocks = [pl.ds(size * m, size) for m in range(parts)]
    loads = [pltpu.make_async_copy(states_ref.at[at], st.at[at], in_sem.at[m]) for m, at in enumerate(blocks)]
    adds = [pltpu.make_async_copy(mean_ref.at[at], mean.at[at], mean_sem.at[m]) for m, at in enumerate(blocks)]
    stores = [pltpu.make_async_copy(st.at[at], new_ref.at[at], out_sem.at[m]) for m, at in enumerate(blocks)]
    for m in range(parts):
        loads[m].start()
        adds[m].start()
    for m, at in enumerate(blocks):
        loads[m].wait()
        adds[m].wait()
        st[at, :] = st[at, :] + mean[at, :].astype(F32)
        stores[m].start()
    for copy in stores:
        copy.wait()


def per_device(
    states,
    row_of_user,
    event_users,
    event_features,
    feature_table,
    gate_in,
    gate_state,
    tower_in,
    tower_out,
):
    table = row_of_user.reshape(2048, 128)
    anywhere = pl.BlockSpec(memory_space=pl.ANY)
    vmem = pl.BlockSpec(memory_space=pltpu.VMEM)
    dma = pltpu.SemaphoreType.DMA
    means, scores = pl.pallas_call(
        kernel,
        out_shape=(
            jax.ShapeDtypeStruct((2048, 512), BF16),
            jax.ShapeDtypeStruct((1, 512), F32),
        ),
        in_specs=[vmem] * 2 + [anywhere] * 7,
        out_specs=(anywhere, vmem),
        scratch_shapes=[
            pltpu.VMEM((2048, 128), jnp.int32),
            pltpu.VMEM((2048, 512), F32),
            pltpu.VMEM((2048, 512), BF16),
            pltpu.VMEM((4096, 512), BF16),
            pltpu.VMEM((512, 1536), BF16),
            pltpu.VMEM((512, 1536), BF16),
            pltpu.VMEM((4, 4, 4, 2, 2, 16, 1024), BF16),
            pltpu.VMEM((4, 4, 2, 16, 4096), BF16),
            pltpu.VMEM((4, 4, 4096), BF16),
            pltpu.VMEM((16, 8, 1, 128), F32),
            pltpu.VMEM((16, 8, 1, 128), F32),
            pltpu.VMEM((8, 16, 1, 128), F32),
            pltpu.VMEM((8, 16, 1, 128), F32),
            pltpu.VMEM((8, 16, 1, 128), F32),
            pltpu.VMEM((16, 8, 1, 128), F32),
            pltpu.VMEM((512, 128), BF16),
            pltpu.VMEM((512, 128), jnp.int32),
            pltpu.VMEM((8, 128, 128), F32),
            pltpu.VMEM((8, 128, 128), F32),
            pltpu.VMEM((8, 1024), F32),
            pltpu.VMEM((1024, 1024), BF16),
            pltpu.VMEM((1024, 512), BF16),
            pltpu.VMEM((1024, 512), BF16),
            pltpu.VMEM((1024, 512), BF16),
            pltpu.VMEM((512, 512), BF16),
            pltpu.VMEM((1024, 4096), BF16),
            pltpu.VMEM((2048, 512), BF16),
            pltpu.VMEM((1024, 128), F32),
            dma((5,)),
            dma((3,)),
            dma((4,)),
            dma((8,)),
            dma((3, 3)),
            dma((3, 3)),
            dma((3, 3)),
            dma((3, 3)),
            dma((3, 6)),
            dma((3, 6)),
            dma((3, 4)),
            dma((3, 4)),
        ],
        compiler_params=pltpu.CompilerParams(
            collective_id=0, has_side_effects=True, vmem_limit_bytes=60 * 1024 * 1024
        ),
    )(event_users.reshape(1, 512), event_features.reshape(1, 512), table, states, feature_table, gate_in, gate_state, tower_in, tower_out)
    new_states = pl.pallas_call(
        update_kernel,
        out_shape=jax.ShapeDtypeStruct((2048, 512), F32),
        in_specs=[anywhere] * 2,
        out_specs=anywhere,
        scratch_shapes=[
            pltpu.VMEM((2048, 512), F32),
            pltpu.VMEM((2048, 512), BF16),
            dma((8,)),
            dma((8,)),
            dma((8,)),
        ],
        compiler_params=pltpu.CompilerParams(vmem_limit_bytes=60 * 1024 * 1024),
    )(states, means)
    return new_states, scores.reshape(512)


def solution(mesh):
    placed = (
        P(AXES, None),
        P(),
        P(AXES),
        P(AXES),
        P(),
        P(),
        P(),
        P(AXES, None),
        P(AXES, None),
    )
    return jax.shard_map(
        per_device,
        mesh=mesh,
        in_specs=placed,
        out_specs=(P(AXES, None), P(AXES)),
        check_vma=False,
    )
```
